128 devices in a mesh: leaf: 64 (over z, y, x), front: 2 (over core).
Axes of the slice: x: 4, y: 4, z: 4, core: 2. Of those that a mesh axis runs over, the one named last changes fastest.
Arguments:
- fac_left: bfloat16 [64, 1536, 512], P('leaf', None, 'front'), may hold values from -6 to 6
- fac_right: bfloat16 [64, 256, 512], P('leaf', None, 'front'), may hold values from -0.21875 to 0.21875
- block_rank: int32 [64, 8], replicated, may hold values from 8 to 64
- col_map: int32 [64, 8], replicated, may hold values from 0 to 15, as said below
- child_lead: bfloat16 [64, 1536, 1536], P('leaf', 'front'), as said below
- orig_lead: bfloat16 [64, 768, 1536], P('leaf', 'front'), as said below
- orig_panel: bfloat16 [64, 1536, 2048], P('leaf', None, 'front'), may hold values from -4 to 4
- orig_next: bfloat16 [64, 512, 2048], P('leaf', None, 'front'), may hold values from -6 to 6
Outputs:
- factor_lead: float32 [64, 768, 1536], P('leaf', 'front')
- upper_panel: float32 [64, 1536, 2048], P('leaf', None, 'front')
- next_panel: float32 [64, 512, 2048], P('leaf', None, 'front')
The draws below stay inside these ranges and needn't reach their ends.
Inputs may be any that keep to these rules, and one draw needn't show every extreme that they name: `col_map`: each child's 8 block columns name distinct parent block columns. `child_lead`: symmetric; with orig_lead it makes each parent's fully summed block positive definite. `orig_lead`: the two row halves of a parent form a symmetric matrix.
All inputs are finite; a program needn't handle non-finite values.
Results may differ from the reference program's by a relative error of at most 0.0049.
Values may be sent and summed in bfloat16 or wider, within the bound.
A program may use at most 192 MiB of HBM per device.

```python
import math
import jax
import jax.numpy as jnp
from jax import lax

BLK = 256
RMAX = 64
FS = 1536
PBLK = 16
CBLK = 8
CHILDREN = 64
HALF = 2048
NEXT = 512


def symmetric_noise(key, count, order):
    values = jax.random.normal(key, (count, order, order), jnp.float32)
    return values + jnp.swapaxes(values, 1, 2)


def draw_col_map(key, part):
    keys = jax.random.split(jax.random.fold_in(key, 7), CHILDREN)
    perms = jax.vmap(lambda single: jax.random.permutation(single, PBLK))(keys)
    return perms[:, :CBLK].astype(jnp.int32)


def draw_child_lead(key, part):
    noise = symmetric_noise(jax.random.fold_in(key, 11), CHILDREN, FS)
    return (noise * (0.35 / math.sqrt(FS))).astype(jnp.bfloat16)


def draw_orig_lead(key, part):
    noise = symmetric_noise(jax.random.fold_in(key, 13), CHILDREN // 2, FS) * (0.35 / math.sqrt(FS))
    level = jax.random.uniform(jax.random.fold_in(key, 17), (CHILDREN // 2, FS), jnp.float32, math.log(4.0), math.log(12.0))
    factors = jax.random.randint(jax.random.fold_in(key, 19), (CHILDREN // 2, FS, 32), -2, 3, jnp.int32)
    coupled = jnp.einsum('pfr,pgr->pfg', factors, factors)
    eye = jnp.eye(FS, dtype=jnp.float32)
    full = noise + jnp.exp(level)[:, :, None] * eye[None] + coupled.astype(jnp.float32) * 0.125
    return full.reshape(CHILDREN, FS // 2, FS).astype(jnp.bfloat16)


def touch_ends(result, stream_key, least, top_value):
    longest = result.shape.index(max(result.shape))
    spots = []
    for shift in (0, 1):
        where = [jax.random.randint(jax.random.fold_in(stream_key, axis), (), 0, length) for axis, length in enumerate(result.shape)]
        where[longest] = (where[longest] + shift) % result.shape[longest]
        spots.append(tuple(where))
    return result.at[spots[0]].set(least).at[spots[1]].set(top_value)


def block_levels(stream_key, extent, shards, smallest, high):
    level = 1.0
    for axis_at, parts in shards:
        steps = jax.random.uniform(jax.random.fold_in(jax.random.fold_in(stream_key, 6), axis_at), (parts,), jnp.float32, smallest / len(shards), high / len(shards))
        level = level * jnp.repeat(jnp.exp(steps), extent[axis_at] // parts).reshape((-1,) + (1,) * (len(extent) - 1 - axis_at))
    return level


def centred(stream_key, dims, scale, most, cuts=(), kind=jnp.bfloat16):
    loudness = block_levels(stream_key, dims, cuts, -0.22, 0.18) if cuts else 1.0
    array = jax.random.normal(stream_key, dims, jnp.float32) * scale * loudness
    return jnp.minimum(jnp.maximum(array, -most), most).astype(kind)


def setup_inputs(seed: int = 0) -> dict:
    arg_keys = jax.random.split(jax.random.key(seed), 9)
    return {
        "fac_left": centred(arg_keys[0], (CHILDREN, FS, CBLK * RMAX), 1.0, 6.0, ((0, 64), (2, 2))),
        "fac_right": centred(arg_keys[1], (CHILDREN, BLK, CBLK * RMAX), (RMAX * 11) ** -0.5, 0.21875, ((0, 64), (2, 2))),
        "block_rank": touch_ends(jax.random.randint(arg_keys[2], (CHILDREN, CBLK), RMAX // 8, RMAX + 1), jax.random.fold_in(arg_keys[2], 1), RMAX // 8, RMAX).astype(jnp.int32),
        "col_map": draw_col_map(jax.random.fold_in(arg_keys[8], 71), 0),
        "child_lead": draw_child_lead(jax.random.fold_in(arg_keys[8], 71), 0),
        "orig_lead": draw_orig_lead(jax.random.fold_in(arg_keys[8], 71), 0),
        "orig_panel": centred(arg_keys[6], (CHILDREN, FS, HALF), 0.3, 4.0, ((0, 64), (2, 2))),
        "orig_next": centred(arg_keys[7], (CHILDREN, NEXT, HALF), 0.5, 6.0, ((0, 64), (2, 2))),
    }


def one_parent(items):
    lefts, rights, ranks, maps, leads, origs, panels, nexts = items
    highest = lax.Precision.HIGHEST
    mask = (jnp.arange(RMAX)[None, None, :] < ranks[:, :, None]).astype(jnp.float32)
    xs_part = lefts.astype(jnp.float32).reshape(2, FS, CBLK, RMAX) * mask[:, None]
    ys_part = rights.astype(jnp.float32).reshape(2, BLK, CBLK, RMAX)
    blocks = jnp.einsum('cfnr,cbnr->cfnb', xs_part, ys_part, precision=highest).astype(jnp.bfloat16)
    select = (maps[:, :, None] == jnp.arange(PBLK)[None, None, :]).astype(jnp.float32)
    spread = jnp.einsum('cnp,cfnb->fpb', select, blocks.astype(jnp.float32), precision=highest)
    panel = jnp.concatenate([panels[0], panels[1]], axis=1).astype(jnp.float32) + spread.reshape(FS, PBLK * BLK)
    lead = leads[0].astype(jnp.float32) + leads[1].astype(jnp.float32)
    lead = lead + jnp.concatenate([origs[0], origs[1]], axis=0).astype(jnp.float32)
    factor = jnp.linalg.cholesky(lead)
    upper = jax.scipy.linalg.solve_triangular(factor, panel, lower=True)
    half_cols = PBLK * BLK // 2
    half_next = NEXT // 2
    leading = jnp.concatenate([upper[:, :half_next], upper[:, half_cols:half_cols + half_next]], axis=1)
    nexts_full = jnp.concatenate([nexts[0], nexts[1]], axis=1).astype(jnp.float32)
    below = nexts_full - jnp.dot(leading.T, upper, precision=highest)
    return (factor.reshape(2, FS // 2, FS), upper.reshape(FS, 2, half_cols).transpose(1, 0, 2), below.reshape(NEXT, 2, half_cols).transpose(1, 0, 2))

def reference(fac_left, fac_right, block_rank, col_map, child_lead, orig_lead, orig_panel, orig_next):
    count = CHILDREN // 2
    items = (fac_left.reshape((count, 2) + fac_left.shape[1:]), fac_right.reshape((count, 2) + fac_right.shape[1:]), block_rank.reshape((count, 2) + block_rank.shape[1:]), col_map.reshape((count, 2) + col_map.shape[1:]), child_lead.reshape((count, 2) + child_lead.shape[1:]), orig_lead.reshape((count, 2) + orig_lead.shape[1:]), orig_panel.reshape((count, 2) + orig_panel.shape[1:]), orig_next.reshape((count, 2) + orig_next.shape[1:]))
    factors, uppers, belows = lax.map(one_parent, items)
    return (factors.reshape((CHILDREN,) + factors.shape[2:]), uppers.reshape((CHILDREN,) + uppers.shape[2:]), belows.reshape((CHILDREN,) + belows.shape[2:]))
```

```python
import functools

import jax
import jax.numpy as jnp
from jax import lax
from jax.experimental import pallas as pl
from jax.experimental.pallas import tpu as pltpu
from jax.sharding import PartitionSpec as P

MESH = pl.DeviceIdType.MESH
F32 = jnp.float32
BF16 = jnp.bfloat16
N = 1536
NB = 256
H = 128
STEPS = N // NB
HALF = N // 2
QUARTER = N // 4
RMAX = 64


def split(x):
    hi = x.astype(BF16)
    return hi, (x - hi.astype(F32)).astype(BF16)


def dot(a, b):
    return jnp.dot(a, b, preferred_element_type=F32)


def dot3(ah, al, bh, bl):
    return dot(ah, bh) + (dot(ah, bl) + dot(al, bh))


def dot_split(a, b):
    return dot3(*split(a), *split(b))


def factor_128(r_ref, x_ref, u_out, x_out):
    sub = lax.broadcasted_iota(jnp.int32, (8, H), 0)

    def panel(p, carry):
        top, rest = r_ref[0:8, :], r_ref[8:H, :]
        xtop, xrest = x_ref[0:8, :], x_ref[8:H, :]
        scale = jnp.ones((8, H), F32)
        for i in range(8):
            ctop = jnp.broadcast_to(top[:, i : i + 1], (8, H))
            crest = jnp.broadcast_to(rest[:, i : i + 1], (H - 8, H))
            pivot = ctop[i : i + 1, :]
            inv = 1.0 / pivot
            row = top[i : i + 1, :] * inv
            xrow = xtop[i : i + 1, :] * inv
            ctop = jnp.where(sub > i, ctop, 0.0)
            scale = jnp.where(sub == i, pivot, scale)
            top = top - ctop * row
            xtop = xtop - ctop * xrow
            rest = rest - crest * row
            xrest = xrest - crest * xrow
        scale = lax.rsqrt(scale)
        rows = pl.ds(pl.multiple_of(p * 8, 8), 8)
        u_out[rows, :] = pltpu.roll(top * scale, p * 8, 1)
        x_out[rows, :] = xtop * scale
        r_ref[0 : H - 8, :] = pltpu.roll(rest, H - 8, 1)
        r_ref[H - 8 : H, :] = jnp.zeros((8, H), F32)
        x_ref[0 : H - 8, :] = xrest
        x_ref[H - 8 : H, :] = jnp.zeros((8, H), F32)
        return carry

    lax.fori_loop(0, H // 8, panel, 0)
    low = lax.broadcasted_iota(jnp.int32, (H, H), 0)
    col = lax.broadcasted_iota(jnp.int32, (H, H), 1)
    u_out[...] = jnp.where(col >= low, u_out[...], 0.0)


def eye():
    low = lax.broadcasted_iota(jnp.int32, (H, H), 0)
    col = lax.broadcasted_iota(jnp.int32, (H, H), 1)
    return jnp.where(col == low, 1.0, 0.0).astype(F32)


def cols(j):
    return pl.ds(pl.multiple_of(j * NB, NB), NB)


def factor_kernel(
    child, orig, fl, fr, op,
    out_lead, lh, ll, xh, xl, flg, frg, opg,
    ca, cb, og, ox, apan, lf, uh, ul, xf, r_ref, w_ref, u_a, x_a, u_b, x_b,
    loc, sib_send, sib_recv, x_send, relay_send, x_recv, out_sem,
):
    leaf, core = lax.axis_index("leaf"), lax.axis_index("front")
    par = lax.rem(leaf, 2)
    sibling = (leaf, 1 - core)
    xpeer = (leaf + 1 - 2 * par, core)
    barrier = pltpu.get_barrier_semaphore()
    for other in (sibling, xpeer):
        pl.semaphore_signal(barrier, inc=1, device_id=other, device_id_type=MESH)
    pl.semaphore_wait(barrier, 2)

    def slot(ref, index, width):
        return ref.at[:, pl.ds(pl.multiple_of(index * width, 128), width)]

    own = []
    for k in range(STEPS):
        own.append((k // 3, child.at[pl.ds(k % 3 * NB, NB), pl.ds(k * NB, N - k * NB)],
                    ca.at[pl.ds(k * NB, NB), pl.ds(k * NB, N - k * NB)]))
    for c in range(2):
        own.append((c, orig, og.at[pl.ds(c * QUARTER, QUARTER), :]))
    for c in range(2):
        own.append((c, fl, slot(flg, 2 * par + c, 256)))
    for c in range(2):
        own.append((c, fr, slot(frg, 2 * par + c, 256)))
    own.append((0, op.at[:, pl.ds(0, NB)], slot(opg, par, NB)))

    cross = []
    for k in range(STEPS):
        there = cb.at[pl.ds(k * NB, NB), pl.ds(k * NB, N - k * NB)]
        cross.append((k // 3, own[k][1], there, there))
    for g in range(6):
        start = g * H
        width = HALF - start
        src = orig.at[pl.ds(g % 3 * H, H), pl.ds(pl.multiple_of(par * HALF + start, 128), width)]
        there = ox.at[pl.ds(start, H), pl.ds(start, width)]
        cross.append((g // 3, src, there, there))
    for c in range(2):
        cross.append((c, fl, slot(flg, 2 * par + c, 256), slot(flg, 2 * (1 - par) + c, 256)))
    for c in range(2):
        cross.append((c, fr, slot(frg, 2 * par + c, 256), slot(frg, 2 * (1 - par) + c, 256)))
    cross.append((0, op.at[:, pl.ds(0, NB)], slot(opg, par, NB), slot(opg, 1 - par, NB)))

    def local(n):
        return pltpu.make_async_copy(own[n][1], own[n][2], loc.at[n])

    def to_sibling(n):
        return pltpu.make_async_remote_copy(own[n][1], own[n][2], sib_send.at[n], sib_recv.at[n],
                                            device_id=sibling, device_id_type=MESH)

    def to_peer(n):
        return pltpu.make_async_remote_copy(cross[n][1], cross[n][2], x_send.at[n], x_recv.at[n],
                                            device_id=xpeer, device_id_type=MESH)

    def relay(n):
        return pltpu.make_async_remote_copy(cross[n][3], cross[n][3], relay_send.at[n], x_recv.at[n],
                                            device_id=sibling, device_id_type=MESH)

    def start_own(n):
        @pl.when(core == own[n][0])
        def _():
            local(n).start()
            to_sibling(n).start()

    def wait_own(n):
        @pl.when(core == own[n][0])
        def _():
            local(n).wait()

        @pl.when(core != own[n][0])
        def _():
            to_sibling(n).wait_recv()

    def start_cross(n):
        @pl.when(core == cross[n][0])
        def _():
            to_peer(n).start()

    def take_cross(n):
        relay(n).wait_recv()

        @pl.when(core == cross[n][0])
        def _():
            relay(n).start()

    fac = (8, 9, 10, 11, 12)
    xfac = (12, 13, 14, 15, 16)
    for n in (0, 6, 7):
        start_own(n)
    for n in (0, 6, 7):
        start_cross(n)
    for n in (1, 2, 3, 4, 5):
        start_own(n)
    for n in (1, 8, 2):
        start_cross(n)
    for k in range(STEPS):
        lf[pl.ds(k * NB, NB), :] = jnp.zeros((NB, N), F32)

    for k in range(STEPS):
        rows = slice(k * NB, (k + 1) * NB)
        wait_own(k)
        if k == 0:
            wait_own(6)
            wait_own(7)
        take_cross(k)
        if k < 3:
            take_cross(6 + 2 * k)
            take_cross(7 + 2 * k)
        if k == 0:
            for n in (9, 10, 11, 3, 4, 5):
                start_cross(n)
            for n in fac:
                start_own(n)
        if k == 1:
            for n in xfac:
                start_cross(n)

        def assemble(lo, hi, piece):
            @pl.loop(lo, hi)
            def _(j):
                both = ca[rows, cols(j)].astype(F32) + cb[rows, cols(j)].astype(F32)
                apan[:, cols(j)] = both + piece(j)

        if k < 3:
            @pl.when(par == 0)
            def _():
                assemble(k, STEPS, lambda j: og[rows, cols(j)].astype(F32))

            @pl.when(par == 1)
            def _():
                assemble(k, 3, lambda j: ox[rows, cols(j)].astype(F32))
                assemble(3, STEPS, lambda j: og[cols(j - 3), rows].astype(F32).T)
        else:
            part = slice(rows.start - HALF, rows.stop - HALF)

            @pl.when(par == 0)
            def _():
                assemble(k, STEPS, lambda j: ox[part, cols(j - 3)].astype(F32))

            @pl.when(par == 1)
            def _():
                assemble(k, STEPS, lambda j: og[part, cols(j)].astype(F32))

        def updated(j):
            block = apan[:, cols(j)]
            if k == 0:
                return block
            done = slice(0, k * NB)
            return block - dot3(lh[rows, done], ll[rows, done], uh[done, cols(j)], ul[done, cols(j)])

        diag = updated(k)
        r_ref[...] = diag[:H, :H]
        w_ref[...] = eye()
        apan[:, rows] = diag
        factor_128(r_ref, w_ref, u_a, x_a)
        xa = x_a[...]
        uab = dot_split(xa, apan[0:H, rows.start + H : rows.stop])
        lba = uab.T
        r_ref[...] = apan[H:NB, rows.start + H : rows.stop] - dot_split(lba, uab)
        w_ref[...] = eye()
        factor_128(r_ref, w_ref, u_b, x_b)
        xf[0:H, 0:H] = xa
        xf[0:H, H:NB] = jnp.zeros((H, H), F32)
        xf[H:NB, 0:H] = -dot_split(x_b[...], dot_split(lba, xa))
        xf[H:NB, H:NB] = x_b[...]
        mid = rows.start + H
        lf[rows.start : mid, rows.start : mid] = u_a[...].T
        lf[mid : rows.stop, rows.start : mid] = lba
        lf[mid : rows.stop, mid : rows.stop] = u_b[...].T
        hi, lo = split(xf[...])
        xh[rows, :] = hi
        xl[rows, :] = lo
        if k < STEPS - 1:
            @pl.loop(k + 1, STEPS)
            def _(j):
                bh, bl = split(updated(j))
                u = dot3(xh[rows, :], xl[rows, :], bh, bl)
                uhi, ulo = split(u)
                uh[rows, cols(j)] = uhi
                ul[rows, cols(j)] = ulo
                t = u.T
                lf[cols(j), rows] = t
                thi, tlo = split(t)
                lh[cols(j), rows] = thi
                ll[cols(j), rows] = tlo

    mine = pl.ds(pl.multiple_of(par * HALF + core * QUARTER, 128), QUARTER)
    write = pltpu.make_async_copy(lf.at[mine, :], out_lead, out_sem)
    write.start()
    for n in xfac:
        take_cross(n)
    for n in fac:
        wait_own(n)
    for n in range(len(own)):
        @pl.when(core == own[n][0])
        def _():
            to_sibling(n).wait_send()
    for n in range(len(cross)):
        @pl.when(core == cross[n][0])
        def _():
            to_peer(n).wait_send()
            relay(n).wait_send()
    write.wait()


def factor_call(child, orig, fl, fr, op):
    any_spec = pl.BlockSpec(memory_space=pl.ANY)
    vmem = pl.BlockSpec(memory_space=pltpu.VMEM)
    dma = pltpu.SemaphoreType.DMA
    return pl.pallas_call(
        factor_kernel,
        out_shape=(
            jax.ShapeDtypeStruct((QUARTER, N), F32),
            jax.ShapeDtypeStruct((N, N), BF16),
            jax.ShapeDtypeStruct((N, N), BF16),
            jax.ShapeDtypeStruct((N, NB), BF16),
            jax.ShapeDtypeStruct((N, NB), BF16),
            jax.ShapeDtypeStruct((N, 1024), BF16),
            jax.ShapeDtypeStruct((NB, 1024), BF16),
            jax.ShapeDtypeStruct((N, 512), BF16),
        ),
        in_specs=[any_spec] * 5,
        out_specs=(any_spec, vmem, vmem, vmem, vmem, any_spec, any_spec, any_spec),
        scratch_shapes=[
            pltpu.VMEM((N, N), BF16),
            pltpu.VMEM((N, N), BF16),
            pltpu.VMEM((HALF, N), BF16),
            pltpu.VMEM((HALF, HALF), BF16),
            pltpu.VMEM((NB, N), F32),
            pltpu.VMEM((N, N), F32),
            pltpu.VMEM((N, N), BF16),
            pltpu.VMEM((N, N), BF16),
            pltpu.VMEM((NB, NB), F32),
        ]
        + [pltpu.VMEM((H, H), F32)] * 6
        + [dma((13,)), dma((13,)), dma((13,)), dma((17,)), dma((17,)), dma((17,)), dma(())],
        compiler_params=pltpu.CompilerParams(
            collective_id=0, has_side_effects=True, vmem_limit_bytes=56 << 20
        ),
        name="factor",
    )(child, orig, fl, fr, op)


def solve_kernel(lh, ll, xh, xl, fl, fr, op, panel, mask, onext, upper, below, rh, rl, wt):
    step = pl.program_id(0)
    width = panel.shape[1]
    right = jnp.concatenate([fr[...] * mask[0, o : o + 1, :] for o in range(width // NB)], axis=0)

    def orig_rows(rows):
        return jnp.where(step == 0, op[rows, :], panel[rows, :]).astype(F32)

    for k in range(STEPS):
        rows = slice(k * NB, (k + 1) * NB)
        acc = orig_rows(rows) + lax.dot_general(
            fl[rows, :], right, (((1,), (1,)), ((), ())), preferred_element_type=F32
        )
        if k > 0:
            done = slice(0, k * NB)
            acc = acc - dot3(lh[rows, done], ll[rows, done], rh[done, :], rl[done, :])
        bh, bl = split(acc)
        u = dot3(xh[rows, :], xl[rows, :], bh, bl)
        uhi, ulo = split(u)
        rh[rows, :] = uhi
        rl[rows, :] = ulo
        upper[rows, :] = u

        @pl.when(step == 0)
        def _():
            wt[:, rows] = u.T.astype(BF16)

    @pl.when(step > 0)
    def _():
        below[...] = onext[...].astype(F32) - dot(wt[...], rh[...])


def solve_call(lh, ll, xh, xl, fl, fr, op, panel, mask, onext):
    width = 512
    count = panel.shape[1] // width

    def whole(x):
        return pl.BlockSpec(x.shape, lambda t: (0, 0), pipeline_mode=pl.Buffered(1))

    def tile(x):
        return pl.BlockSpec((x.shape[0], width), lambda t: (0, jnp.maximum(t - 1, 0)))

    return pl.pallas_call(
        solve_kernel,
        grid=(count + 1,),
        out_shape=(
            jax.ShapeDtypeStruct(panel.shape, F32),
            jax.ShapeDtypeStruct(onext.shape, F32),
        ),
        in_specs=[whole(x) for x in (lh, ll, xh, xl, fl, fr, op)]
        + [tile(panel), pl.BlockSpec((1, 2, 1024), lambda t: (t, 0, 0)), tile(onext)],
        out_specs=(tile(panel), tile(onext)),
        scratch_shapes=[
            pltpu.VMEM((N, width), BF16),
            pltpu.VMEM((N, width), BF16),
            pltpu.VMEM((512, N), BF16),
        ],
        compiler_params=pltpu.CompilerParams(vmem_limit_bytes=56 << 20),
        name="solve",
    )(lh, ll, xh, xl, fl, fr, op, panel, mask, onext)


def shards(fac_left, fac_right, block_rank, col_map, child_lead, orig_lead, orig_panel, orig_next):
    leaf, core = lax.axis_index("leaf"), lax.axis_index("front")
    par = leaf % 2
    out_lead, lh, ll, xh, xl, flg, frg, opg = factor_call(
        child_lead[0], orig_lead[0], fac_left[0], fac_right[0], orig_panel[0]
    )
    own = par * 8 + core * 4 + jnp.arange(4, dtype=jnp.int32)
    targets = jnp.concatenate([jnp.array([0, 8], jnp.int32), own])
    maps = lax.dynamic_slice_in_dim(col_map, leaf - par, 2, 0).reshape(16)
    ranks = lax.dynamic_slice_in_dim(block_rank, leaf - par, 2, 0).reshape(16)
    live = jnp.arange(RMAX)[None, :] < ranks[:, None]
    hit = targets[:, None] == maps[None, :]
    mask = (hit[:, :, None] & live[None]).astype(BF16).reshape(3, 2, 1024)
    upper, below = solve_call(lh, ll, xh, xl, flg, frg, opg, orig_panel[0], mask, orig_next[0])
    return (out_lead[None], upper[None], below[None])


def solution(mesh):
    placed = (
        P("leaf", None, "front"),
        P("leaf", None, "front"),
        P(),
        P(),
        P("leaf", "front", None),
        P("leaf", "front", None),
        P("leaf", None, "front"),
        P("leaf", None, "front"),
    )
    return jax.shard_map(
        shards,
        mesh=mesh,
        in_specs=placed,
        out_specs=(P("leaf", "front", None), P("leaf", None, "front"), P("leaf", None, "front")),
        check_vma=False,
    )
```

```python
import functools

import jax
import jax.numpy as jnp
from jax import lax
from jax.experimental import pallas as pl
from jax.experimental.pallas import tpu as pltpu
from jax.sharding import PartitionSpec as P

MESH = pl.DeviceIdType.MESH
F32 = jnp.float32
BF16 = jnp.bfloat16
N = 1536
NB = 256
H = 128
STEPS = N // NB
HALF = N // 2
QUARTER = N // 4
RMAX = 64
W = 32


def split(x):
    hi = x.astype(BF16)
    return hi, (x - hi.astype(F32)).astype(BF16)


def dot(a, b):
    return jnp.dot(a, b, preferred_element_type=F32)


def dot3(ah, al, bh, bl):
    return dot(ah, bh) + (dot(ah, bl) + dot(al, bh))


def dot_split(a, b):
    return dot3(*split(a), *split(b))


def factor_128(r_ref, x_ref, u_out, x_out):
    sub = lax.broadcasted_iota(jnp.int32, (W, H), 0)

    def panel(p, carry):
        top, xtop = r_ref[0:W, :], x_ref[0:W, :]
        col = [jnp.broadcast_to(top[k // 8 * 8 :, k : k + 1], (W - k // 8 * 8, H)) for k in range(W)]
        pivots = jnp.ones((W, H), F32)
        inverses = jnp.ones((W, H), F32)
        for i in range(W):
            base = i // 8 * 8
            pivot = col[i][i - base : i - base + 1, :]
            inv = 1.0 / pivot
            m = jnp.where(sub[base:] > i, col[i] * inv, 0.0)
            pivots = jnp.where(sub == i, pivot, pivots)
            inverses = jnp.where(sub == i, inv, inverses)
            for k in range(i + 1, W):
                low = k // 8 * 8
                col[k] = col[k] - m[low - base :] * col[i][k - base : k - base + 1, :]
            row, xrow = top[i : i + 1, :], xtop[i : i + 1, :]
            ntop, nxtop = top[base:] - m * row, xtop[base:] - m * xrow
            top = ntop if base == 0 else jnp.concatenate([top[:base], ntop], axis=0)
            xtop = nxtop if base == 0 else jnp.concatenate([xtop[:base], nxtop], axis=0)
        scale = lax.rsqrt(pivots)
        rows = pl.ds(pl.multiple_of(p * W, W), W)
        u_out[rows, :] = pltpu.roll(top * scale, p * W, 1)
        x_out[rows, :] = xtop * scale
        th, tl = split(top)
        vh, vl = split(jnp.concatenate([top * inverses, xtop * inverses], axis=1))
        update = lax.dot_general(
            jnp.concatenate([th, th, tl], axis=0),
            jnp.concatenate([vh, vl, vh], axis=0),
            (((0,), (0,)), ((), ())),
            preferred_element_type=F32,
        )
        r_ref[0 : H - W, :] = pltpu.roll(r_ref[W:H, :] - update[W:, :H], H - W, 1)
        r_ref[H - W : H, :] = jnp.zeros((W, H), F32)
        x_ref[0 : H - W, :] = x_ref[W:H, :] - update[W:, H:]
        x_ref[H - W : H, :] = jnp.zeros((W, H), F32)
        return carry

    lax.fori_loop(0, H // W, panel, 0)
    low = lax.broadcasted_iota(jnp.int32, (H, H), 0)
    right = lax.broadcasted_iota(jnp.int32, (H, H), 1)
    u_out[...] = jnp.where(right >= low, u_out[...], 0.0)


def eye():
    low = lax.broadcasted_iota(jnp.int32, (H, H), 0)
    col = lax.broadcasted_iota(jnp.int32, (H, H), 1)
    return jnp.where(col == low, 1.0, 0.0).astype(F32)


def cols(j):
    return pl.ds(pl.multiple_of(j * NB, NB), NB)


def factor_kernel(
    child, orig, fl, fr, op,
    out_lead, lh, ll, xh, xl, flg, frg, opg,
    ca, cb, og, ox, apan, lf, uh, ul, xf, r_ref, w_ref, u_a, x_a, u_b, x_b,
    loc, sib_send, sib_recv, x_send, relay_send, x_recv, out_sem,
):
    leaf, core = lax.axis_index("leaf"), lax.axis_index("front")
    par = lax.rem(leaf, 2)
    sibling = (leaf, 1 - core)
    xpeer = (leaf + 1 - 2 * par, core)
    barrier = pltpu.get_barrier_semaphore()
    for other in (sibling, xpeer):
        pl.semaphore_signal(barrier, inc=1, device_id=other, device_id_type=MESH)
    pl.semaphore_wait(barrier, 2)

    def slot(ref, index, width):
        return ref.at[:, pl.ds(pl.multiple_of(index * width, 128), width)]

    own = []
    for k in range(STEPS):
        own.append((k // 3, child.at[pl.ds(k % 3 * NB, NB), pl.ds(k * NB, N - k * NB)],
                    ca.at[pl.ds(k * NB, NB), pl.ds(k * NB, N - k * NB)]))
    for c in range(2):
        own.append((c, orig, og.at[pl.ds(c * QUARTER, QUARTER), :]))
    for c in range(2):
        own.append((c, fl, slot(flg, 2 * par + c, 256)))
    for c in range(2):
        own.append((c, fr, slot(frg, 2 * par + c, 256)))
    own.append((0, op.at[:, pl.ds(0, NB)], slot(opg, par, NB)))

    cross = []
    for k in range(STEPS):
        there = cb.at[pl.ds(k * NB, NB), pl.ds(k * NB, N - k * NB)]
        cross.append((k // 3, own[k][1], there, there))
    for g in range(6):
        start = g * H
        width = HALF - start
        src = orig.at[pl.ds(g % 3 * H, H), pl.ds(pl.multiple_of(par * HALF + start, 128), width)]
        there = ox.at[pl.ds(start, H), pl.ds(start, width)]
        cross.append((g // 3, src, there, there))
    for c in range(2):
        cross.append((c, fl, slot(flg, 2 * par + c, 256), slot(flg, 2 * (1 - par) + c, 256)))
    for c in range(2):
        cross.append((c, fr, slot(frg, 2 * par + c, 256), slot(frg, 2 * (1 - par) + c, 256)))
    cross.append((0, op.at[:, pl.ds(0, NB)], slot(opg, par, NB), slot(opg, 1 - par, NB)))

    def local(n):
        return pltpu.make_async_copy(own[n][1], own[n][2], loc.at[n])

    def to_sibling(n):
        return pltpu.make_async_remote_copy(own[n][1], own[n][2], sib_send.at[n], sib_recv.at[n],
                                            device_id=sibling, device_id_type=MESH)

    def to_peer(n):
        return pltpu.make_async_remote_copy(cross[n][1], cross[n][2], x_send.at[n], x_recv.at[n],
                                            device_id=xpeer, device_id_type=MESH)

    def relay(n):
        return pltpu.make_async_remote_copy(cross[n][3], cross[n][3], relay_send.at[n], x_recv.at[n],
                                            device_id=sibling, device_id_type=MESH)

    def start_own(n):
        @pl.when(core == own[n][0])
        def _():
            local(n).start()
            to_sibling(n).start()

    def wait_own(n):
        @pl.when(core == own[n][0])
        def _():
            local(n).wait()

        @pl.when(core != own[n][0])
        def _():
            to_sibling(n).wait_recv()

    def start_cross(n):
        @pl.when(core == cross[n][0])
        def _():
            to_peer(n).start()

    def take_cross(n):
        relay(n).wait_recv()

        @pl.when(core == cross[n][0])
        def _():
            relay(n).start()

    fac = (8, 9, 10, 11, 12)
    xfac = (12, 13, 14, 15, 16)
    for n in (0, 6, 7):
        start_own(n)
    for n in (0, 6, 7):
        start_cross(n)
    for n in (1, 2, 3, 4, 5):
        start_own(n)
    for n in (1, 8, 2):
        start_cross(n)
    for k in range(STEPS):
        lf[pl.ds(k * NB, NB), :] = jnp.zeros((NB, N), F32)

    for k in range(STEPS):
        rows = slice(k * NB, (k + 1) * NB)
        wait_own(k)
        if k == 0:
            wait_own(6)
            wait_own(7)
        take_cross(k)
        if k < 3:
            take_cross(6 + 2 * k)
            take_cross(7 + 2 * k)
        if k == 0:
            for n in (9, 10, 11, 3, 4, 5):
                start_cross(n)
            for n in fac:
                start_own(n)
        if k == 1:
            for n in xfac:
                start_cross(n)

        def assemble(lo, hi, piece):
            @pl.loop(lo, hi)
            def _(j):
                both = ca[rows, cols(j)].astype(F32) + cb[rows, cols(j)].astype(F32)
                apan[:, cols(j)] = both + piece(j)

        if k < 3:
            @pl.when(par == 0)
            def _():
                assemble(k, STEPS, lambda j: og[rows, cols(j)].astype(F32))

            @pl.when(par == 1)
            def _():
                assemble(k, 3, lambda j: ox[rows, cols(j)].astype(F32))
                assemble(3, STEPS, lambda j: og[cols(j - 3), rows].astype(F32).T)
        else:
            part = slice(rows.start - HALF, rows.stop - HALF)

            @pl.when(par == 0)
            def _():
                assemble(k, STEPS, lambda j: ox[part, cols(j - 3)].astype(F32))

            @pl.when(par == 1)
            def _():
                assemble(k, STEPS, lambda j: og[part, cols(j)].astype(F32))

        def updated(j):
            block = apan[:, cols(j)]
            if k == 0:
                return block
            done = slice(0, k * NB)
            return block - dot3(lh[rows, done], ll[rows, done], uh[done, cols(j)], ul[done, cols(j)])

        diag = updated(k)
        r_ref[...] = diag[:H, :H]
        w_ref[...] = eye()
        apan[:, rows] = diag
        factor_128(r_ref, w_ref, u_a, x_a)
        xa = x_a[...]
        uab = dot_split(xa, apan[0:H, rows.start + H : rows.stop])
        lba = uab.T
        r_ref[...] = apan[H:NB, rows.start + H : rows.stop] - dot_split(lba, uab)
        w_ref[...] = eye()
        factor_128(r_ref, w_ref, u_b, x_b)
        xf[0:H, 0:H] = xa
        xf[0:H, H:NB] = jnp.zeros((H, H), F32)
        xf[H:NB, 0:H] = -dot_split(x_b[...], dot_split(lba, xa))
        xf[H:NB, H:NB] = x_b[...]
        mid = rows.start + H
        lf[rows.start : mid, rows.start : mid] = u_a[...].T
        lf[mid : rows.stop, rows.start : mid] = lba
        lf[mid : rows.stop, mid : rows.stop] = u_b[...].T
        hi, lo = split(xf[...])
        xh[rows, :] = hi
        xl[rows, :] = lo
        if k < STEPS - 1:
            @pl.loop(k + 1, STEPS)
            def _(j):
                bh, bl = split(updated(j))
                u = dot3(xh[rows, :], xl[rows, :], bh, bl)
                uhi, ulo = split(u)
                uh[rows, cols(j)] = uhi
                ul[rows, cols(j)] = ulo
                t = u.T
                lf[cols(j), rows] = t
                thi, tlo = split(t)
                lh[cols(j), rows] = thi
                ll[cols(j), rows] = tlo

    mine = pl.ds(pl.multiple_of(par * HALF + core * QUARTER, 128), QUARTER)
    write = pltpu.make_async_copy(lf.at[mine, :], out_lead, out_sem)
    write.start()
    for n in xfac:
        take_cross(n)
    for n in fac:
        wait_own(n)
    for n in range(len(own)):
        @pl.when(core == own[n][0])
        def _():
            to_sibling(n).wait_send()
    for n in range(len(cross)):
        @pl.when(core == cross[n][0])
        def _():
            to_peer(n).wait_send()
            relay(n).wait_send()
    write.wait()


def factor_call(child, orig, fl, fr, op):
    any_spec = pl.BlockSpec(memory_space=pl.ANY)
    vmem = pl.BlockSpec(memory_space=pltpu.VMEM)
    dma = pltpu.SemaphoreType.DMA
    return pl.pallas_call(
        factor_kernel,
        out_shape=(
            jax.ShapeDtypeStruct((QUARTER, N), F32),
            jax.ShapeDtypeStruct((N, N), BF16),
            jax.ShapeDtypeStruct((N, N), BF16),
            jax.ShapeDtypeStruct((N, NB), BF16),
            jax.ShapeDtypeStruct((N, NB), BF16),
            jax.ShapeDtypeStruct((N, 1024), BF16),
            jax.ShapeDtypeStruct((NB, 1024), BF16),
            jax.ShapeDtypeStruct((N, 512), BF16),
        ),
        in_specs=[any_spec] * 5,
        out_specs=(any_spec, vmem, vmem, vmem, vmem, any_spec, any_spec, any_spec),
        scratch_shapes=[
            pltpu.VMEM((N, N), BF16),
            pltpu.VMEM((N, N), BF16),
            pltpu.VMEM((HALF, N), BF16),
            pltpu.VMEM((HALF, HALF), BF16),
            pltpu.VMEM((NB, N), F32),
            pltpu.VMEM((N, N), F32),
            pltpu.VMEM((N, N), BF16),
            pltpu.VMEM((N, N), BF16),
            pltpu.VMEM((NB, NB), F32),
        ]
        + [pltpu.VMEM((H, H), F32)] * 6
        + [dma((13,)), dma((13,)), dma((13,)), dma((17,)), dma((17,)), dma((17,)), dma(())],
        compiler_params=pltpu.CompilerParams(
            collective_id=0, has_side_effects=True, vmem_limit_bytes=56 << 20
        ),
        name="factor",
    )(child, orig, fl, fr, op)


def solve_kernel(lh, ll, xh, xl, fl, fr, op, panel, mask, onext, upper, below, rh, rl, wt):
    step = pl.program_id(0)
    width = panel.shape[1]
    right = jnp.concatenate([fr[...] * mask[0, o : o + 1, :] for o in range(width // NB)], axis=0)

    def orig_rows(rows):
        return jnp.where(step == 0, op[rows, :], panel[rows, :]).astype(F32)

    for k in range(STEPS):
        rows = slice(k * NB, (k + 1) * NB)
        acc = orig_rows(rows) + lax.dot_general(
            fl[rows, :], right, (((1,), (1,)), ((), ())), preferred_element_type=F32
        )
        if k > 0:
            done = slice(0, k * NB)
            acc = acc - dot3(lh[rows, done], ll[rows, done], rh[done, :], rl[done, :])
        bh, bl = split(acc)
        u = dot3(xh[rows, :], xl[rows, :], bh, bl)
        uhi, ulo = split(u)
        rh[rows, :] = uhi
        rl[rows, :] = ulo
        upper[rows, :] = u

        @pl.when(step == 0)
        def _():
            wt[:, rows] = u.T.astype(BF16)

    @pl.when(step > 0)
    def _():
        below[...] = onext[...].astype(F32) - dot(wt[...], rh[...])


def solve_call(lh, ll, xh, xl, fl, fr, op, panel, mask, onext):
    width = 512
    count = panel.shape[1] // width

    def whole(x):
        return pl.BlockSpec(x.shape, lambda t: (0, 0), pipeline_mode=pl.Buffered(1))

    def tile(x):
        return pl.BlockSpec((x.shape[0], width), lambda t: (0, jnp.maximum(t - 1, 0)))

    return pl.pallas_call(
        solve_kernel,
        grid=(count + 1,),
        out_shape=(
            jax.ShapeDtypeStruct(panel.shape, F32),
            jax.ShapeDtypeStruct(onext.shape, F32),
        ),
        in_specs=[whole(x) for x in (lh, ll, xh, xl, fl, fr, op)]
        + [tile(panel), pl.BlockSpec((1, 2, 1024), lambda t: (t, 0, 0)), tile(onext)],
        out_specs=(tile(panel), tile(onext)),
        scratch_shapes=[
            pltpu.VMEM((N, width), BF16),
            pltpu.VMEM((N, width), BF16),
            pltpu.VMEM((512, N), BF16),
        ],
        compiler_params=pltpu.CompilerParams(vmem_limit_bytes=56 << 20),
        name="solve",
    )(lh, ll, xh, xl, fl, fr, op, panel, mask, onext)


def shards(fac_left, fac_right, block_rank, col_map, child_lead, orig_lead, orig_panel, orig_next):
    leaf, core = lax.axis_index("leaf"), lax.axis_index("front")
    par = leaf % 2
    out_lead, lh, ll, xh, xl, flg, frg, opg = factor_call(
        child_lead[0], orig_lead[0], fac_left[0], fac_right[0], orig_panel[0]
    )
    own = par * 8 + core * 4 + jnp.arange(4, dtype=jnp.int32)
    targets = jnp.concatenate([jnp.array([0, 8], jnp.int32), own])
    maps = lax.dynamic_slice_in_dim(col_map, leaf - par, 2, 0).reshape(16)
    ranks = lax.dynamic_slice_in_dim(block_rank, leaf - par, 2, 0).reshape(16)
    live = jnp.arange(RMAX)[None, :] < ranks[:, None]
    hit = targets[:, None] == maps[None, :]
    mask = (hit[:, :, None] & live[None]).astype(BF16).reshape(3, 2, 1024)
    upper, below = solve_call(lh, ll, xh, xl, flg, frg, opg, orig_panel[0], mask, orig_next[0])
    return (out_lead[None], upper[None], below[None])


def solution(mesh):
    placed = (
        P("leaf", None, "front"),
        P("leaf", None, "front"),
        P(),
        P(),
        P("leaf", "front", None),
        P("leaf", "front", None),
        P("leaf", None, "front"),
        P("leaf", None, "front"),
    )
    return jax.shard_map(
        shards,
        mesh=mesh,
        in_specs=placed,
        out_specs=(P("leaf", "front", None), P("leaf", None, "front"), P("leaf", None, "front")),
        check_vma=False,
    )
```

```python
import functools

import jax
import jax.numpy as jnp
from jax import lax
from jax.experimental import pallas as pl
from jax.experimental.pallas import tpu as pltpu
from jax.sharding import PartitionSpec as P

MESH = pl.DeviceIdType.MESH
F32 = jnp.float32
BF16 = jnp.bfloat16
N = 1536
NB = 256
H = 128
STEPS = N // NB
HALF = N // 2
QUARTER = N // 4
RMAX = 64
W = 32


def split(x):
    hi = x.astype(BF16)
    return hi, (x - hi.astype(F32)).astype(BF16)


def dot(a, b):
    return jnp.dot(a, b, preferred_element_type=F32)


def dot3(ah, al, bh, bl):
    return dot(ah, bh) + (dot(ah, bl) + dot(al, bh))


def dot_split(a, b):
    return dot3(*split(a), *split(b))


def factor_128(r_ref, x_ref, u_out, x_out):
    sub = lax.broadcasted_iota(jnp.int32, (W, H), 0)

    def panel(p, carry):
        top, xtop = r_ref[0:W, :], x_ref[0:W, :]
        col = [jnp.broadcast_to(top[k // 8 * 8 :, k : k + 1], (W - k // 8 * 8, H)) for k in range(W)]
        pivots = jnp.ones((W, H), F32)
        inverses = jnp.ones((W, H), F32)
        for i in range(W):
            base = i // 8 * 8
            pivot = col[i][i - base : i - base + 1, :]
            inv = 1.0 / pivot
            m = jnp.where(sub[base:] > i, col[i] * inv, 0.0)
            pivots = jnp.where(sub == i, pivot, pivots)
            inverses = jnp.where(sub == i, inv, inverses)
            for k in range(i + 1, W):
                low = k // 8 * 8
                col[k] = col[k] - m[low - base :] * col[i][k - base : k - base + 1, :]
            row, xrow = top[i : i + 1, :], xtop[i : i + 1, :]
            ntop, nxtop = top[base:] - m * row, xtop[base:] - m * xrow
            top = ntop if base == 0 else jnp.concatenate([top[:base], ntop], axis=0)
            xtop = nxtop if base == 0 else jnp.concatenate([xtop[:base], nxtop], axis=0)
        scale = lax.rsqrt(pivots)
        rows = pl.ds(pl.multiple_of(p * W, W), W)
        u_out[rows, :] = pltpu.roll(top * scale, p * W, 1)
        x_out[rows, :] = xtop * scale
        th, tl = split(top)
        vh, vl = split(jnp.concatenate([top * inverses, xtop * inverses], axis=1))
        update = lax.dot_general(
            jnp.concatenate([th, th, tl], axis=0),
            jnp.concatenate([vh, vl, vh], axis=0),
            (((0,), (0,)), ((), ())),
            preferred_element_type=F32,
        )
        r_ref[0 : H - W, :] = pltpu.roll(r_ref[W:H, :] - update[W:, :H], H - W, 1)
        r_ref[H - W : H, :] = jnp.zeros((W, H), F32)
        x_ref[0 : H - W, :] = x_ref[W:H, :] - update[W:, H:]
        x_ref[H - W : H, :] = jnp.zeros((W, H), F32)
        return carry

    lax.fori_loop(0, H // W, panel, 0)
    low = lax.broadcasted_iota(jnp.int32, (H, H), 0)
    right = lax.broadcasted_iota(jnp.int32, (H, H), 1)
    u_out[...] = jnp.where(right >= low, u_out[...], 0.0)


def eye():
    low = lax.broadcasted_iota(jnp.int32, (H, H), 0)
    col = lax.broadcasted_iota(jnp.int32, (H, H), 1)
    return jnp.where(col == low, 1.0, 0.0).astype(F32)


def cols(j):
    return pl.ds(pl.multiple_of(j * NB, NB), NB)


def factor_kernel(
    child, orig, fl, fr, op,
    out_lead, lh_out, ll_out, xh, xl, flg, frg, opg,
    ca, cb, og, ox, apan, lf, lh, ll, uh, ul, xf, r_ref, w_ref, u_a, x_a, u_b, x_b,
    loc, sib_send, sib_recv, x_send, relay_send, x_recv, out_sem,
):
    leaf, core = lax.axis_index("leaf"), lax.axis_index("front")
    par = lax.rem(leaf, 2)
    sibling = (leaf, 1 - core)
    xpeer = (leaf + 1 - 2 * par, core)
    barrier = pltpu.get_barrier_semaphore()
    for other in (sibling, xpeer):
        pl.semaphore_signal(barrier, inc=1, device_id=other, device_id_type=MESH)
    pl.semaphore_wait(barrier, 2)

    def slot(ref, index, width):
        return ref.at[:, pl.ds(pl.multiple_of(index * width, 128), width)]

    def box(ref, row, height, col, width):
        return ref.at[pl.ds(row, height), pl.ds(col, width)]

    own = [
        (0, box(child, 0, NB, 0, NB), box(ca, 0, NB, 0, NB)),
        (0, box(orig, 0, NB, 0, NB), box(og, 0, NB, 0, NB)),
        (0, box(child, 0, NB, NB, N - NB), box(ca, 0, NB, NB, N - NB)),
        (0, box(orig, 0, NB, NB, N - NB), box(og, 0, NB, NB, N - NB)),
        (0, box(orig, NB, H, 0, N), box(og, NB, H, 0, N)),
        (1, orig, box(og, QUARTER, QUARTER, 0, N)),
    ]
    for k in range(1, STEPS):
        own.append((k // 3, box(child, k % 3 * NB, NB, k * NB, N - k * NB), box(ca, k * NB, NB, k * NB, N - k * NB)))
    for c in range(2):
        own.append((c, fl, slot(flg, 2 * par + c, 256)))
    for c in range(2):
        own.append((c, fr, slot(frg, 2 * par + c, 256)))
    own.append((0, op.at[:, pl.ds(0, NB)], slot(opg, par, NB)))

    def square(c, row, height, start, width):
        src = box(orig, row, height, pl.multiple_of(par * HALF + start, 128), width)
        there = box(ox, c * QUARTER + row, height, start, width)
        return (c, src, there, there)

    def lead_item(k, start, width):
        src = box(child, k % 3 * NB, NB, start, width)
        there = box(cb, k * NB, NB, start, width)
        return (k // 3, src, there, there)

    cross = [
        lead_item(0, 0, NB),
        square(0, 0, NB, 0, NB),
        lead_item(0, NB, N - NB),
        square(0, 0, NB, NB, HALF - NB),
        lead_item(1, NB, N - NB),
        square(0, NB, H, NB, HALF - NB),
        square(1, 0, H, QUARTER, QUARTER),
        lead_item(2, 2 * NB, N - 2 * NB),
        square(1, H, H, QUARTER + H, QUARTER - H),
        square(1, 2 * H, H, QUARTER + 2 * H, H),
    ]
    for k in range(3, STEPS):
        cross.append(lead_item(k, k * NB, N - k * NB))
    for c in range(2):
        cross.append((c, fl, slot(flg, 2 * par + c, 256), slot(flg, 2 * (1 - par) + c, 256)))
    for c in range(2):
        cross.append((c, fr, slot(frg, 2 * par + c, 256), slot(frg, 2 * (1 - par) + c, 256)))
    cross.append((0, op.at[:, pl.ds(0, NB)], slot(opg, par, NB), slot(opg, 1 - par, NB)))

    def local(n):
        return pltpu.make_async_copy(own[n][1], own[n][2], loc.at[n])

    def to_sibling(n):
        return pltpu.make_async_remote_copy(own[n][1], own[n][2], sib_send.at[n], sib_recv.at[n],
                                            device_id=sibling, device_id_type=MESH)

    def to_peer(n):
        return pltpu.make_async_remote_copy(cross[n][1], cross[n][2], x_send.at[n], x_recv.at[n],
                                            device_id=xpeer, device_id_type=MESH)

    def relay(n):
        return pltpu.make_async_remote_copy(cross[n][3], cross[n][3], relay_send.at[n], x_recv.at[n],
                                            device_id=sibling, device_id_type=MESH)

    def start_own(*items):
        for n in items:
            @pl.when(core == own[n][0])
            def _():
                local(n).start()
                to_sibling(n).start()

    def wait_own(*items):
        for n in items:
            @pl.when(core == own[n][0])
            def _():
                local(n).wait()

            @pl.when(core != own[n][0])
            def _():
                to_sibling(n).wait_recv()

    def start_cross(*items):
        for n in items:
            @pl.when(core == cross[n][0])
            def _():
                to_peer(n).start()

    def take_cross(*items):
        for n in items:
            relay(n).wait_recv()

            @pl.when(core == cross[n][0])
            def _():
                relay(n).start()

    start_cross(0, 1)
    start_own(0, 1, 2, 3, 4, 5)
    for k in range(STEPS):
        lf[pl.ds(k * NB, NB), :] = jnp.zeros((NB, N), F32)
    wait_own(0, 1)
    take_cross(0, 1)
    start_cross(2, 3)
    start_own(6, 7, 8, 9, 10)

    arrivals = {1: (4, 5, 6), 2: (7, 8, 9), 3: (10,), 4: (11,), 5: (12,)}
    writes = []
    for k in range(STEPS):
        rows = slice(k * NB, (k + 1) * NB)
        if k > 0:
            wait_own(5 + k)
            take_cross(*arrivals[k])
        if k == 1:
            start_cross(7, 8, 9)
        if k == 2:
            start_cross(15, 16, 17)

        def assemble(lo, hi, piece):
            @pl.loop(lo, hi)
            def _(j):
                both = ca[rows, cols(j)].astype(F32) + cb[rows, cols(j)].astype(F32)
                apan[:, cols(j)] = both + piece(j)

        def assemble_all(lo, hi):
            if k < 3:
                @pl.when(par == 0)
                def _():
                    assemble(lo, hi, lambda j: og[rows, cols(j)].astype(F32))

                @pl.when(par == 1)
                def _():
                    assemble(lo, min(hi, 3), lambda j: ox[rows, cols(j)].astype(F32))
                    if hi > 3:
                        assemble(3, hi, lambda j: og[cols(j - 3), rows].astype(F32).T)
            else:
                part = slice(rows.start - HALF, rows.stop - HALF)

                @pl.when(par == 0)
                def _():
                    assemble(lo, hi, lambda j: ox[part, cols(j - 3)].astype(F32))

                @pl.when(par == 1)
                def _():
                    assemble(lo, hi, lambda j: og[part, cols(j)].astype(F32))

        assemble_all(k, STEPS if k > 0 else 1)

        def updated(j):
            block = apan[:, cols(j)]
            if k == 0:
                return block
            done = slice(0, k * NB)
            return block - dot3(lh[rows, done], ll[rows, done], uh[done, cols(j)], ul[done, cols(j)])

        diag = updated(k)
        r_ref[...] = diag[:H, :H]
        w_ref[...] = eye()
        apan[:, rows] = diag
        factor_128(r_ref, w_ref, u_a, x_a)
        if k == 1:
            start_cross(10)
        if k == 5:
            take_cross(13, 14, 15, 16, 17)
        xa = x_a[...]
        uab = dot_split(xa, apan[0:H, rows.start + H : rows.stop])
        lba = uab.T
        r_ref[...] = apan[H:NB, rows.start + H : rows.stop] - dot_split(lba, uab)
        w_ref[...] = eye()
        factor_128(r_ref, w_ref, u_b, x_b)
        if k == 0:
            start_cross(4, 5, 6)
            wait_own(2, 3, 4, 5)
            take_cross(2, 3)
            assemble_all(1, STEPS)
            start_own(11, 12, 13, 14, 15)
        if k == 1:
            start_cross(11, 12, 13, 14)
        xf[0:H, 0:H] = xa
        xf[0:H, H:NB] = jnp.zeros((H, H), F32)
        xf[H:NB, 0:H] = -dot_split(x_b[...], dot_split(lba, xa))
        xf[H:NB, H:NB] = x_b[...]
        mid = rows.start + H
        lf[rows.start : mid, rows.start : mid] = u_a[...].T
        lf[mid : rows.stop, rows.start : mid] = lba
        lf[mid : rows.stop, mid : rows.stop] = u_b[...].T
        hi, lo = split(xf[...])
        xh[rows, :] = hi
        xl[rows, :] = lo
        if k < STEPS - 1:
            @pl.loop(k + 1, STEPS)
            def _(j):
                bh, bl = split(updated(j))
                u = dot3(xh[rows, :], xl[rows, :], bh, bl)
                uhi, ulo = split(u)
                uh[rows, cols(j)] = uhi
                ul[rows, cols(j)] = ulo
                t = u.T
                lf[cols(j), rows] = t
                thi, tlo = split(t)
                lh[cols(j), rows] = thi
                ll[cols(j), rows] = tlo

            below = rows.stop
            for ref, dst in ((lh, lh_out), (ll, ll_out)):
                copy = pltpu.make_async_copy(
                    box(ref, below, N - below, rows.start, NB),
                    box(dst, below, N - below, rows.start, NB),
                    out_sem.at[len(writes)],
                )
                copy.start()
                writes.append(copy)

    mine = pl.ds(pl.multiple_of(par * HALF + core * QUARTER, 128), QUARTER)
    write = pltpu.make_async_copy(lf.at[mine, :], out_lead, out_sem.at[len(writes)])
    write.start()
    writes.append(write)
    wait_own(11, 12, 13, 14, 15)
    for n in range(len(own)):
        @pl.when(core == own[n][0])
        def _():
            to_sibling(n).wait_send()
    for n in range(len(cross)):
        @pl.when(core == cross[n][0])
        def _():
            to_peer(n).wait_send()
            relay(n).wait_send()
    for copy in writes:
        copy.wait()


def factor_call(child, orig, fl, fr, op):
    any_spec = pl.BlockSpec(memory_space=pl.ANY)
    vmem = pl.BlockSpec(memory_space=pltpu.VMEM)
    dma = pltpu.SemaphoreType.DMA
    return pl.pallas_call(
        factor_kernel,
        out_shape=(
            jax.ShapeDtypeStruct((QUARTER, N), F32),
            jax.ShapeDtypeStruct((N, N), BF16),
            jax.ShapeDtypeStruct((N, N), BF16),
            jax.ShapeDtypeStruct((N, NB), BF16),
            jax.ShapeDtypeStruct((N, NB), BF16),
            jax.ShapeDtypeStruct((N, 1024), BF16),
            jax.ShapeDtypeStruct((NB, 1024), BF16),
            jax.ShapeDtypeStruct((N, 512), BF16),
        ),
        in_specs=[any_spec] * 5,
        out_specs=(any_spec, any_spec, any_spec, vmem, vmem, any_spec, any_spec, any_spec),
        scratch_shapes=[
            pltpu.VMEM((N, N), BF16),
            pltpu.VMEM((N, N), BF16),
            pltpu.VMEM((HALF, N), BF16),
            pltpu.VMEM((HALF, HALF), BF16),
            pltpu.VMEM((NB, N), F32),
            pltpu.VMEM((N, N), F32),
            pltpu.VMEM((N, N), BF16),
            pltpu.VMEM((N, N), BF16),
            pltpu.VMEM((N, N), BF16),
            pltpu.VMEM((N, N), BF16),
            pltpu.VMEM((NB, NB), F32),
        ]
        + [pltpu.VMEM((H, H), F32)] * 6
        + [dma((16,)), dma((16,)), dma((16,)), dma((18,)), dma((18,)), dma((18,)), dma((11,))],
        compiler_params=pltpu.CompilerParams(
            collective_id=0, has_side_effects=True, vmem_limit_bytes=56 << 20
        ),
        name="factor",
    )(child, orig, fl, fr, op)


def solve_kernel(
    place, lh_in, ll_in, fl_in, op_in, xh, xl, fr, panel, mask, onext, upper, below,
    lh, ll, fl, op, rh, wt, sems,
):
    step = pl.program_id(0)
    width = panel.shape[1]

    def loads(k):
        rows = pl.ds(k * NB, NB)
        pairs = [(fl_in.at[rows, :], fl.at[rows, :]), (op_in.at[rows, :], op.at[rows, :])]
        if k > 0:
            done = pl.ds(0, k * NB)
            pairs += [(lh_in.at[rows, done], lh.at[rows, done]), (ll_in.at[rows, done], ll.at[rows, done])]
        return [pltpu.make_async_copy(src, dst, sems.at[k, n]) for n, (src, dst) in enumerate(pairs)]

    @pl.when(step == 0)
    def _():
        for k in range(STEPS):
            for copy in loads(k):
                copy.start()

    spots, rights = [], []
    for o in range(width // NB):
        spot = [pl.ds(pl.multiple_of(place[step, 2 * o + c] * H, H), H) for c in range(2)]
        spots.append(spot)
        rights.append(jnp.concatenate([fr[:, s] * mask[0, o : o + 1, c * H : c * H + H] for c, s in enumerate(spot)], axis=1))

    for k in range(STEPS):
        rows = slice(k * NB, (k + 1) * NB)

        @pl.when(step == 0)
        def _():
            for copy in loads(k):
                copy.wait()

        spread = jnp.concatenate(
            [
                lax.dot_general(
                    jnp.concatenate([fl[rows, s] for s in spot], axis=1),
                    right,
                    (((1,), (1,)), ((), ())),
                    preferred_element_type=F32,
                )
                for spot, right in zip(spots, rights)
            ],
            axis=1,
        )
        acc = jnp.where(step == 0, op[rows, :], panel[rows, :]).astype(F32) + spread
        if k > 0:
            done = slice(0, k * NB)
            acc = acc - (dot(lh[rows, done], rh[done, :]) + dot(ll[rows, done], rh[done, :]))
        bh, bl = split(acc)
        u = dot3(xh[rows, :], xl[rows, :], bh, bl)
        rh[rows, :] = u.astype(BF16)
        upper[rows, :] = u

        @pl.when(step == 0)
        def _():
            wt[:, rows] = u.T.astype(BF16)

    @pl.when(step > 0)
    def _():
        below[...] = onext[...].astype(F32) - dot(wt[...], rh[...])


def solve_call(place, lh, ll, xh, xl, fl, fr, op, panel, mask, onext):
    width = 512
    count = panel.shape[1] // width
    any_spec = pl.BlockSpec(memory_space=pl.ANY)

    def whole(x):
        return pl.BlockSpec(x.shape, lambda t, p: (0, 0), pipeline_mode=pl.Buffered(1))

    def tile(x):
        return pl.BlockSpec((x.shape[0], width), lambda t, p: (0, jnp.maximum(t - 1, 0)))

    return pl.pallas_call(
        solve_kernel,
        out_shape=(
            jax.ShapeDtypeStruct(panel.shape, F32),
            jax.ShapeDtypeStruct(onext.shape, F32),
        ),
        grid_spec=pltpu.PrefetchScalarGridSpec(
            num_scalar_prefetch=1,
            grid=(count + 1,),
            in_specs=[any_spec] * 4
            + [whole(x) for x in (xh, xl, fr)]
            + [tile(panel), pl.BlockSpec((1, 2, 2 * H), lambda t, p: (t, 0, 0)), tile(onext)],
            out_specs=(tile(panel), tile(onext)),
            scratch_shapes=[
                pltpu.VMEM((N, N), BF16),
                pltpu.VMEM((N, N), BF16),
                pltpu.VMEM((N, 1024), BF16),
                pltpu.VMEM((N, 512), BF16),
                pltpu.VMEM((N, width), BF16),
                pltpu.VMEM((512, N), BF16),
                pltpu.SemaphoreType.DMA((STEPS, 4)),
            ],
        ),
        compiler_params=pltpu.CompilerParams(vmem_limit_bytes=56 << 20),
        name="solve",
    )(place, lh, ll, fl, op, xh, xl, fr, panel, mask, onext)


def shards(fac_left, fac_right, block_rank, col_map, child_lead, orig_lead, orig_panel, orig_next):
    leaf, core = lax.axis_index("leaf"), lax.axis_index("front")
    par = leaf % 2
    out_lead, lh, ll, xh, xl, flg, frg, opg = factor_call(
        child_lead[0], orig_lead[0], fac_left[0], fac_right[0], orig_panel[0]
    )
    own = par * 8 + core * 4 + jnp.arange(4, dtype=jnp.int32)
    targets = jnp.concatenate([jnp.array([0, 8], jnp.int32), own])
    maps = lax.dynamic_slice_in_dim(col_map, leaf - par, 2, 0).reshape(16)
    ranks = lax.dynamic_slice_in_dim(block_rank, leaf - par, 2, 0).reshape(16)
    hit = (targets[:, None] == maps[None, :]).reshape(6, 2, 8)
    pair = jnp.sum(jnp.where(hit, jnp.arange(8, dtype=jnp.int32) // 2, 0), axis=2)
    place = (pair + jnp.array([[0, 4]], jnp.int32)).reshape(3, 4)
    live = (jnp.arange(RMAX)[None, :] < ranks[:, None]).reshape(1, 2, 8, RMAX)
    used = (hit[..., None] & live).reshape(6, 2, 4, 2 * RMAX)
    mask = jnp.any(used, axis=2).astype(BF16).reshape(3, 2, 4 * RMAX)
    upper, below = solve_call(place, lh, ll, xh, xl, flg, frg, opg, orig_panel[0], mask, orig_next[0])
    return (out_lead[None], upper[None], below[None])


def solution(mesh):
    placed = (
        P("leaf", None, "front"),
        P("leaf", None, "front"),
        P(),
        P(),
        P("leaf", "front", None),
        P("leaf", "front", None),
        P("leaf", None, "front"),
        P("leaf", None, "front"),
    )
    return jax.shard_map(
        shards,
        mesh=mesh,
        in_specs=placed,
        out_specs=(P("leaf", "front", None), P("leaf", None, "front"), P("leaf", None, "front")),
        check_vma=False,
    )
```

```python
import functools

import jax
import jax.numpy as jnp
from jax import lax
from jax.experimental import pallas as pl
from jax.experimental.pallas import tpu as pltpu
from jax.sharding import PartitionSpec as P

MESH = pl.DeviceIdType.MESH
F32 = jnp.float32
BF16 = jnp.bfloat16
N = 1536
NB = 256
H = 128
STEPS = N // NB
HALF = N // 2
QUARTER = N // 4
RMAX = 64
W = 32


def split(x):
    hi = x.astype(BF16)
    return hi, (x - hi.astype(F32)).astype(BF16)


def dot(a, b):
    return jnp.dot(a, b, preferred_element_type=F32)


def dot3(ah, al, bh, bl):
    return dot(ah, bh) + (dot(ah, bl) + dot(al, bh))


def dot_split(a, b):
    return dot3(*split(a), *split(b))


def factor_128(r_ref, x_ref, u_out, x_out):
    sub = lax.broadcasted_iota(jnp.int32, (W, H), 0)

    def panel(p, carry):
        top, xtop = r_ref[0:W, :], x_ref[0:W, :]
        col = [jnp.broadcast_to(top[k // 8 * 8 :, k : k + 1], (W - k // 8 * 8, H)) for k in range(W)]
        pivots = jnp.ones((W, H), F32)
        inverses = jnp.ones((W, H), F32)
        for i in range(W):
            base = i // 8 * 8
            pivot = col[i][i - base : i - base + 1, :]
            inv = 1.0 / pivot
            m = jnp.where(sub[base:] > i, col[i] * inv, 0.0)
            pivots = jnp.where(sub == i, pivot, pivots)
            inverses = jnp.where(sub == i, inv, inverses)
            for k in range(i + 1, W):
                low = k // 8 * 8
                col[k] = col[k] - m[low - base :] * col[i][k - base : k - base + 1, :]
            row, xrow = top[i : i + 1, :], xtop[i : i + 1, :]
            ntop, nxtop = top[base:] - m * row, xtop[base:] - m * xrow
            top = ntop if base == 0 else jnp.concatenate([top[:base], ntop], axis=0)
            xtop = nxtop if base == 0 else jnp.concatenate([xtop[:base], nxtop], axis=0)
        scale = lax.rsqrt(pivots)
        rows = pl.ds(pl.multiple_of(p * W, W), W)
        u_out[rows, :] = pltpu.roll(top * scale, p * W, 1)
        x_out[rows, :] = xtop * scale
        th, tl = split(top)
        vh, vl = split(jnp.concatenate([top * inverses, xtop * inverses], axis=1))
        update = lax.dot_general(
            jnp.concatenate([th, th, tl], axis=0),
            jnp.concatenate([vh, vl, vh], axis=0),
            (((0,), (0,)), ((), ())),
            preferred_element_type=F32,
        )
        r_ref[0 : H - W, :] = pltpu.roll(r_ref[W:H, :] - update[W:, :H], H - W, 1)
        r_ref[H - W : H, :] = jnp.zeros((W, H), F32)
        x_ref[0 : H - W, :] = x_ref[W:H, :] - update[W:, H:]
        x_ref[H - W : H, :] = jnp.zeros((W, H), F32)
        return carry

    lax.fori_loop(0, H // W, panel, 0)
    low = lax.broadcasted_iota(jnp.int32, (H, H), 0)
    right = lax.broadcasted_iota(jnp.int32, (H, H), 1)
    u_out[...] = jnp.where(right >= low, u_out[...], 0.0)


def eye():
    low = lax.broadcasted_iota(jnp.int32, (H, H), 0)
    col = lax.broadcasted_iota(jnp.int32, (H, H), 1)
    return jnp.where(col == low, 1.0, 0.0).astype(F32)


def factor_kernel(
    child, orig, fl, fr, op,
    out_lead, lh_out, ll_out, xh, xl, flg, frg, opg,
    ca, cb, og, ox, acol, lf, lh, ll, uh, ul, xf, r_ref, w_ref, u_a, x_a, u_b, x_b,
    loc, sib_send, sib_recv, x_send, relay_send, x_recv, out_sem,
):
    leaf, core = lax.axis_index("leaf"), lax.axis_index("front")
    par = lax.rem(leaf, 2)
    sibling = (leaf, 1 - core)
    xpeer = (leaf + 1 - 2 * par, core)
    barrier = pltpu.get_barrier_semaphore()
    for other in (sibling, xpeer):
        pl.semaphore_signal(barrier, inc=1, device_id=other, device_id_type=MESH)
    pl.semaphore_wait(barrier, 2)

    def slot(ref, index, width):
        return ref.at[:, pl.ds(pl.multiple_of(index * width, 128), width)]

    def box(ref, row, height, col, width):
        return ref.at[pl.ds(row, height), pl.ds(col, width)]

    own = [
        (0, box(orig, 0, NB, 0, NB), box(og, 0, NB, 0, NB)),
        (0, box(orig, 0, NB, NB, N - NB), box(og, 0, NB, NB, N - NB)),
        (0, box(orig, NB, H, 0, N), box(og, NB, H, 0, N)),
        (1, orig, box(og, QUARTER, QUARTER, 0, N)),
    ]
    own_col, cross_col, cross = [], [], []
    for k in range(STEPS):
        own_col.append([len(own)])
        high = min(NB * (k + 1), HALF)
        own.append((0, box(child, 0, high, k * NB, NB), box(ca, 0, high, k * NB, NB)))
        if k >= 3:
            own_col[k].append(len(own))
            own.append((1, box(child, 0, NB * (k - 2), k * NB, NB), box(ca, HALF, NB * (k - 2), k * NB, NB)))
    own_fac = tuple(range(len(own), len(own) + 5))
    for c in range(2):
        own.append((c, fl, slot(flg, 2 * par + c, 256)))
    for c in range(2):
        own.append((c, fr, slot(frg, 2 * par + c, 256)))
    own.append((0, op.at[:, pl.ds(0, NB)], slot(opg, par, NB)))

    def square(c, height, k):
        src = box(orig, 0, height, pl.multiple_of(par * HALF + k * NB, 128), NB)
        there = box(ox, c * QUARTER, height, k * NB, NB)
        cross_col[k].append(len(cross))
        cross.append((c, src, there, there))

    for k in range(STEPS):
        high = min(NB * (k + 1), HALF)
        cross_col.append([len(cross)])
        there = box(cb, 0, high, k * NB, NB)
        cross.append((0, box(child, 0, high, k * NB, NB), there, there))
        if k >= 3:
            there = box(cb, HALF, NB * (k - 2), k * NB, NB)
            cross_col[k].append(len(cross))
            cross.append((1, box(child, 0, NB * (k - 2), k * NB, NB), there, there))
        else:
            square(0, min(NB * (k + 1), QUARTER), k)
            if k > 0:
                square(1, NB * (k + 1) - QUARTER, k)
    first = len(cross)
    for c in range(2):
        cross.append((c, fl, slot(flg, 2 * par + c, 256), slot(flg, 2 * (1 - par) + c, 256)))
    for c in range(2):
        cross.append((c, fr, slot(frg, 2 * par + c, 256), slot(frg, 2 * (1 - par) + c, 256)))
    cross.append((0, op.at[:, pl.ds(0, NB)], slot(opg, par, NB), slot(opg, 1 - par, NB)))
    cross_fl, cross_rest = (first, first + 1), (first + 2, first + 3, first + 4)

    def local(n):
        return pltpu.make_async_copy(own[n][1], own[n][2], loc.at[n])

    def to_sibling(n):
        return pltpu.make_async_remote_copy(own[n][1], own[n][2], sib_send.at[n], sib_recv.at[n],
                                            device_id=sibling, device_id_type=MESH)

    def to_peer(n):
        return pltpu.make_async_remote_copy(cross[n][1], cross[n][2], x_send.at[n], x_recv.at[n],
                                            device_id=xpeer, device_id_type=MESH)

    def relay(n):
        return pltpu.make_async_remote_copy(cross[n][3], cross[n][3], relay_send.at[n], x_recv.at[n],
                                            device_id=sibling, device_id_type=MESH)

    def start_own(*items):
        for n in items:
            @pl.when(core == own[n][0])
            def _():
                local(n).start()
                to_sibling(n).start()

    def wait_own(*items):
        for n in items:
            @pl.when(core == own[n][0])
            def _():
                local(n).wait()

            @pl.when(core != own[n][0])
            def _():
                to_sibling(n).wait_recv()

    def start_cross(*items):
        for n in items:
            @pl.when(core == cross[n][0])
            def _():
                to_peer(n).start()

    def pass_on(*items):
        for n in items:
            @pl.when(core == cross[n][0])
            def _():
                relay(n).wait_recv()
                relay(n).start()

    def take(*items):
        for n in items:
            @pl.when(core != cross[n][0])
            def _():
                relay(n).wait_recv()

    start_cross(*cross_col[0])
    start_own(0, *own_col[0])
    for k in range(STEPS):
        lf[pl.ds(k * NB, NB), :] = jnp.zeros((NB, N), F32)
    pass_on(*cross_col[0])
    start_cross(*cross_col[1])
    start_own(1, 2, 3)
    for k in range(1, STEPS):
        start_own(*own_col[k])

    writes = []
    for k in range(STEPS):
        rows = slice(k * NB, (k + 1) * NB)
        wait_own(*own_col[k])
        wait_own(*{0: (0,), 1: (1, 2, 3)}.get(k, ()))
        take(*cross_col[k])
        if k == 1:
            start_cross(*cross_col[4])
        if k == 2:
            start_cross(*cross_fl)
            start_own(*own_fac)
        if k == 3:
            start_cross(*cross_rest)

        def assemble(lo, hi, piece):
            for i in range(lo, hi):
                part = slice(i * NB, (i + 1) * NB)
                both = ca[part, rows].astype(F32) + cb[part, rows].astype(F32)
                acol[part, :] = both + piece(i)

        def lower(ref, i, j):
            return ref[i * NB : (i + 1) * NB, j * NB : (j + 1) * NB].astype(F32)

        @pl.when(par == 0)
        def _():
            assemble(0, min(k + 1, 3), lambda i: lower(og, i, k))
            assemble(3, k + 1, lambda i: lower(ox, i - 3, k - 3))

        @pl.when(par == 1)
        def _():
            if k < 3:
                assemble(0, k + 1, lambda i: lower(ox, i, k))
            else:
                assemble(0, 3, lambda i: lower(og, k - 3, i).T)
                assemble(3, k + 1, lambda i: lower(og, i - 3, k))

        def updated(i):
            part = slice(i * NB, (i + 1) * NB)
            if i == 0:
                return acol[part, :]
            done = slice(0, i * NB)
            return acol[part, :] - dot3(lh[part, done], ll[part, done], uh[done, :], ul[done, :])

        for i in range(k):
            part = slice(i * NB, (i + 1) * NB)
            bh, bl = split(updated(i))
            u = dot3(xh[part, :], xl[part, :], bh, bl)
            uhi, ulo = split(u)
            uh[part, :] = uhi
            ul[part, :] = ulo
            t = u.T
            lf[rows, part] = t
            thi, tlo = split(t)
            lh[rows, part] = thi
            ll[rows, part] = tlo
        if k > 0:
            for ref, dst in ((lh, lh_out), (ll, ll_out)):
                copy = pltpu.make_async_copy(
                    box(ref, rows.start, NB, 0, k * NB),
                    box(dst, rows.start, NB, 0, k * NB),
                    out_sem.at[len(writes)],
                )
                copy.start()
                writes.append(copy)

        diag = updated(k)
        acol[rows, :] = diag
        r_ref[...] = diag[:H, :H]
        w_ref[...] = eye()
        factor_128(r_ref, w_ref, u_a, x_a)
        if k == 0:
            start_cross(*cross_col[2])
        if k == 1:
            start_cross(*cross_col[5])
        if k < STEPS - 1:
            pass_on(*cross_col[k + 1])
        if k == STEPS - 1:
            pass_on(*cross_fl)
        mid = rows.start + H
        xa = x_a[...]
        uab = dot_split(xa, acol[rows.start : mid, H:NB])
        lba = uab.T
        r_ref[...] = acol[mid : rows.stop, H:NB] - dot_split(lba, uab)
        w_ref[...] = eye()
        factor_128(r_ref, w_ref, u_b, x_b)
        if k == 0:
            start_cross(*cross_col[3])
        if k == STEPS - 1:
            pass_on(*cross_rest)
        xf[0:H, 0:H] = xa
        xf[0:H, H:NB] = jnp.zeros((H, H), F32)
        xf[H:NB, 0:H] = -dot_split(x_b[...], dot_split(lba, xa))
        xf[H:NB, H:NB] = x_b[...]
        lf[rows.start : mid, rows.start : mid] = u_a[...].T
        lf[mid : rows.stop, rows.start : mid] = lba
        lf[mid : rows.stop, mid : rows.stop] = u_b[...].T
        hi, lo = split(xf[...])
        xh[rows, :] = hi
        xl[rows, :] = lo

    mine = pl.ds(pl.multiple_of(par * HALF + core * QUARTER, 128), QUARTER)
    write = pltpu.make_async_copy(lf.at[mine, :], out_lead, out_sem.at[len(writes)])
    write.start()
    writes.append(write)
    wait_own(*own_fac)
    take(*cross_fl, *cross_rest)
    for n in range(len(own)):
        @pl.when(core == own[n][0])
        def _():
            to_sibling(n).wait_send()
    for n in range(len(cross)):
        @pl.when(core == cross[n][0])
        def _():
            to_peer(n).wait_send()
            relay(n).wait_send()
    for copy in writes:
        copy.wait()


def factor_call(child, orig, fl, fr, op):
    any_spec = pl.BlockSpec(memory_space=pl.ANY)
    vmem = pl.BlockSpec(memory_space=pltpu.VMEM)
    dma = pltpu.SemaphoreType.DMA
    return pl.pallas_call(
        factor_kernel,
        out_shape=(
            jax.ShapeDtypeStruct((QUARTER, N), F32),
            jax.ShapeDtypeStruct((N, N), BF16),
            jax.ShapeDtypeStruct((N, N), BF16),
            jax.ShapeDtypeStruct((N, NB), BF16),
            jax.ShapeDtypeStruct((N, NB), BF16),
            jax.ShapeDtypeStruct((N, 1024), BF16),
            jax.ShapeDtypeStruct((NB, 1024), BF16),
            jax.ShapeDtypeStruct((N, 512), BF16),
        ),
        in_specs=[any_spec] * 5,
        out_specs=(any_spec, any_spec, any_spec, vmem, vmem, any_spec, any_spec, any_spec),
        scratch_shapes=[
            pltpu.VMEM((N, N), BF16),
            pltpu.VMEM((N, N), BF16),
            pltpu.VMEM((HALF, N), BF16),
            pltpu.VMEM((HALF, HALF), BF16),
            pltpu.VMEM((N, NB), F32),
            pltpu.VMEM((N, N), F32),
            pltpu.VMEM((N, N), BF16),
            pltpu.VMEM((N, N), BF16),
            pltpu.VMEM((N, NB), BF16),
            pltpu.VMEM((N, NB), BF16),
            pltpu.VMEM((NB, NB), F32),
        ]
        + [pltpu.VMEM((H, H), F32)] * 6
        + [dma((18,)), dma((18,)), dma((18,)), dma((19,)), dma((19,)), dma((19,)), dma((11,))],
        compiler_params=pltpu.CompilerParams(
            collective_id=0, has_side_effects=True, vmem_limit_bytes=56 << 20
        ),
        name="factor",
    )(child, orig, fl, fr, op)


def solve_kernel(
    place, lh_in, ll_in, fl_in, op_in, xh, xl, fr, panel, mask, onext, upper, below,
    lh, ll, fl, op, rh, wt, sems,
):
    step = pl.program_id(0)
    width = panel.shape[1]

    def loads(k):
        rows = pl.ds(k * NB, NB)
        pairs = [(fl_in.at[rows, :], fl.at[rows, :]), (op_in.at[rows, :], op.at[rows, :])]
        if k > 0:
            done = pl.ds(0, k * NB)
            pairs += [(lh_in.at[rows, done], lh.at[rows, done]), (ll_in.at[rows, done], ll.at[rows, done])]
        return [pltpu.make_async_copy(src, dst, sems.at[k, n]) for n, (src, dst) in enumerate(pairs)]

    @pl.when(step == 0)
    def _():
        for k in range(STEPS):
            for copy in loads(k):
                copy.start()

    spots, rights = [], []
    for o in range(width // NB):
        spot = [pl.ds(pl.multiple_of(place[step, 2 * o + c] * H, H), H) for c in range(2)]
        spots.append(spot)
        rights.append(jnp.concatenate([fr[:, s] * mask[0, o : o + 1, c * H : c * H + H] for c, s in enumerate(spot)], axis=1))

    for k in range(STEPS):
        rows = slice(k * NB, (k + 1) * NB)

        @pl.when(step == 0)
        def _():
            for copy in loads(k):
                copy.wait()

        spread = jnp.concatenate(
            [
                lax.dot_general(
                    jnp.concatenate([fl[rows, s] for s in spot], axis=1),
                    right,
                    (((1,), (1,)), ((), ())),
                    preferred_element_type=F32,
                )
                for spot, right in zip(spots, rights)
            ],
            axis=1,
        )
        acc = jnp.where(step == 0, op[rows, :], panel[rows, :]).astype(F32) + spread
        if k > 0:
            done = slice(0, k * NB)
            acc = acc - (dot(lh[rows, done], rh[done, :]) + dot(ll[rows, done], rh[done, :]))
        bh, bl = split(acc)
        u = dot3(xh[rows, :], xl[rows, :], bh, bl)
        rh[rows, :] = u.astype(BF16)
        upper[rows, :] = u

        @pl.when(step == 0)
        def _():
            wt[:, rows] = u.T.astype(BF16)

    @pl.when(step > 0)
    def _():
        below[...] = onext[...].astype(F32) - dot(wt[...], rh[...])


def solve_call(place, lh, ll, xh, xl, fl, fr, op, panel, mask, onext):
    width = 512
    count = panel.shape[1] // width
    any_spec = pl.BlockSpec(memory_space=pl.ANY)

    def whole(x):
        return pl.BlockSpec(x.shape, lambda t, p: (0, 0), pipeline_mode=pl.Buffered(1))

    def tile(x):
        return pl.BlockSpec((x.shape[0], width), lambda t, p: (0, jnp.maximum(t - 1, 0)))

    return pl.pallas_call(
        solve_kernel,
        out_shape=(
            jax.ShapeDtypeStruct(panel.shape, F32),
            jax.ShapeDtypeStruct(onext.shape, F32),
        ),
        grid_spec=pltpu.PrefetchScalarGridSpec(
            num_scalar_prefetch=1,
            grid=(count + 1,),
            in_specs=[any_spec] * 4
            + [whole(x) for x in (xh, xl, fr)]
            + [tile(panel), pl.BlockSpec((1, 2, 2 * H), lambda t, p: (t, 0, 0)), tile(onext)],
            out_specs=(tile(panel), tile(onext)),
            scratch_shapes=[
                pltpu.VMEM((N, N), BF16),
                pltpu.VMEM((N, N), BF16),
                pltpu.VMEM((N, 1024), BF16),
                pltpu.VMEM((N, 512), BF16),
                pltpu.VMEM((N, width), BF16),
                pltpu.VMEM((512, N), BF16),
                pltpu.SemaphoreType.DMA((STEPS, 4)),
            ],
        ),
        compiler_params=pltpu.CompilerParams(vmem_limit_bytes=56 << 20),
        name="solve",
    )(place, lh, ll, fl, op, xh, xl, fr, panel, mask, onext)


def shards(fac_left, fac_right, block_rank, col_map, child_lead, orig_lead, orig_panel, orig_next):
    leaf, core = lax.axis_index("leaf"), lax.axis_index("front")
    par = leaf % 2
    out_lead, lh, ll, xh, xl, flg, frg, opg = factor_call(
        child_lead[0], orig_lead[0], fac_left[0], fac_right[0], orig_panel[0]
    )
    own = par * 8 + core * 4 + jnp.arange(4, dtype=jnp.int32)
    targets = jnp.concatenate([jnp.array([0, 8], jnp.int32), own])
    maps = lax.dynamic_slice_in_dim(col_map, leaf - par, 2, 0).reshape(16)
    ranks = lax.dynamic_slice_in_dim(block_rank, leaf - par, 2, 0).reshape(16)
    hit = (targets[:, None] == maps[None, :]).reshape(6, 2, 8)
    pair = jnp.sum(jnp.where(hit, jnp.arange(8, dtype=jnp.int32) // 2, 0), axis=2)
    place = (pair + jnp.array([[0, 4]], jnp.int32)).reshape(3, 4)
    live = (jnp.arange(RMAX)[None, :] < ranks[:, None]).reshape(1, 2, 8, RMAX)
    used = (hit[..., None] & live).reshape(6, 2, 4, 2 * RMAX)
    mask = jnp.any(used, axis=2).astype(BF16).reshape(3, 2, 4 * RMAX)
    upper, below = solve_call(place, lh, ll, xh, xl, flg, frg, opg, orig_panel[0], mask, orig_next[0])
    return (out_lead[None], upper[None], below[None])


def solution(mesh):
    placed = (
        P("leaf", None, "front"),
        P("leaf", None, "front"),
        P(),
        P(),
        P("leaf", "front", None),
        P("leaf", "front", None),
        P("leaf", None, "front"),
        P("leaf", None, "front"),
    )
    return jax.shard_map(
        shards,
        mesh=mesh,
        in_specs=placed,
        out_specs=(P("leaf", "front", None), P("leaf", None, "front"), P("leaf", None, "front")),
        check_vma=False,
    )
```

```python
import functools

import jax
import jax.numpy as jnp
from jax import lax
from jax.experimental import pallas as pl
from jax.experimental.pallas import tpu as pltpu
from jax.sharding import PartitionSpec as P

MESH = pl.DeviceIdType.MESH
F32 = jnp.float32
BF16 = jnp.bfloat16
N = 1536
NB = 256
H = 128
STEPS = N // NB
HALF = N // 2
QUARTER = N // 4
RMAX = 64
W = 32


def split(x):
    hi = x.astype(BF16)
    return hi, (x - hi.astype(F32)).astype(BF16)


def dot(a, b):
    return jnp.dot(a, b, preferred_element_type=F32)


def dot3(ah, al, bh, bl):
    return dot(ah, bh) + (dot(ah, bl) + dot(al, bh))


def dot_split(a, b):
    return dot3(*split(a), *split(b))


def factor_128(r_ref, x_ref, u_out, x_out, held):
    sub = lax.broadcasted_iota(jnp.int32, (W, H), 0)

    def panel(p, carry):
        top, xtop = r_ref[0:W, :], x_ref[0:W, :]
        col = [jnp.broadcast_to(top[k // 8 * 8 :, k : k + 1], (W - k // 8 * 8, H)) for k in range(W)]
        pivots = jnp.ones((W, H), F32)
        inverses = jnp.ones((W, H), F32)
        for i in range(W):
            base = i // 8 * 8
            held[i * W + base : (i + 1) * W, :] = col[i]
            pivot = col[i][i - base : i - base + 1, :]
            inv = 1.0 / pivot
            m = jnp.where(sub[base:] > i, col[i] * inv, 0.0)
            pivots = jnp.where(sub == i, pivot, pivots)
            inverses = jnp.where(sub == i, inv, inverses)
            for k in range(i + 1, W):
                low = k // 8 * 8
                near = col[i][k - base : k - base + 1, :] if k == i + 1 else held[i * W + k : i * W + k + 1, :]
                col[k] = col[k] - m[low - base :] * near
            row, xrow = top[i : i + 1, :], xtop[i : i + 1, :]
            ntop, nxtop = top[base:] - m * row, xtop[base:] - m * xrow
            top = ntop if base == 0 else jnp.concatenate([top[:base], ntop], axis=0)
            xtop = nxtop if base == 0 else jnp.concatenate([xtop[:base], nxtop], axis=0)
        scale = lax.rsqrt(pivots)
        rows = pl.ds(pl.multiple_of(p * W, W), W)
        u_out[rows, :] = pltpu.roll(top * scale, p * W, 1)
        x_out[rows, :] = xtop * scale
        th, tl = split(top)
        vh, vl = split(jnp.concatenate([top * inverses, xtop * inverses], axis=1))
        update = lax.dot_general(
            jnp.concatenate([th, th, tl], axis=0),
            jnp.concatenate([vh, vl, vh], axis=0),
            (((0,), (0,)), ((), ())),
            preferred_element_type=F32,
        )
        r_ref[0 : H - W, :] = pltpu.roll(r_ref[W:H, :] - update[W:, :H], H - W, 1)
        r_ref[H - W : H, :] = jnp.zeros((W, H), F32)
        x_ref[0 : H - W, :] = x_ref[W:H, :] - update[W:, H:]
        x_ref[H - W : H, :] = jnp.zeros((W, H), F32)
        return carry

    lax.fori_loop(0, H // W, panel, 0)
    low = lax.broadcasted_iota(jnp.int32, (H, H), 0)
    right = lax.broadcasted_iota(jnp.int32, (H, H), 1)
    u_out[...] = jnp.where(right >= low, u_out[...], 0.0)


def eye():
    low = lax.broadcasted_iota(jnp.int32, (H, H), 0)
    col = lax.broadcasted_iota(jnp.int32, (H, H), 1)
    return jnp.where(col == low, 1.0, 0.0).astype(F32)


def factor_kernel(
    child, orig, fl, fr, op,
    out_lead, lh_out, ll_out, xh, xl, flg, frg, opg,
    ca, cb, og, ox, acol, lf, lh, ll, uh, ul, xf, r_ref, w_ref, u_a, x_a, u_b, x_b, held,
    loc, sib_send, sib_recv, x_send, relay_send, x_recv, out_sem,
):
    leaf, core = lax.axis_index("leaf"), lax.axis_index("front")
    par = lax.rem(leaf, 2)
    sibling = (leaf, 1 - core)
    xpeer = (leaf + 1 - 2 * par, core)
    barrier = pltpu.get_barrier_semaphore()
    for other in (sibling, xpeer):
        pl.semaphore_signal(barrier, inc=1, device_id=other, device_id_type=MESH)
    pl.semaphore_wait(barrier, 2)

    def slot(ref, index, width):
        return ref.at[:, pl.ds(pl.multiple_of(index * width, 128), width)]

    def box(ref, row, height, col, width):
        return ref.at[pl.ds(row, height), pl.ds(col, width)]

    own = [
        (0, box(orig, 0, NB, 0, NB), box(og, 0, NB, 0, NB)),
        (0, box(orig, 0, NB, NB, N - NB), box(og, 0, NB, NB, N - NB)),
        (0, box(orig, NB, H, 0, N), box(og, NB, H, 0, N)),
        (1, orig, box(og, QUARTER, QUARTER, 0, N)),
    ]
    own_col, cross_col, cross = [], [], []
    for k in range(STEPS):
        own_col.append([len(own)])
        high = min(NB * (k + 1), HALF)
        own.append((0, box(child, 0, high, k * NB, NB), box(ca, 0, high, k * NB, NB)))
        if k >= 3:
            own_col[k].append(len(own))
            own.append((1, box(child, 0, NB * (k - 2), k * NB, NB), box(ca, HALF, NB * (k - 2), k * NB, NB)))
    own_fac = tuple(range(len(own), len(own) + 5))
    for c in range(2):
        own.append((c, fl, slot(flg, 2 * par + c, 256)))
    for c in range(2):
        own.append((c, fr, slot(frg, 2 * par + c, 256)))
    own.append((0, op.at[:, pl.ds(0, NB)], slot(opg, par, NB)))

    def square(c, height, k):
        src = box(orig, 0, height, pl.multiple_of(par * HALF + k * NB, 128), NB)
        there = box(ox, c * QUARTER, height, k * NB, NB)
        cross_col[k].append(len(cross))
        cross.append((c, src, there, there))

    for k in range(STEPS):
        high = min(NB * (k + 1), HALF)
        cross_col.append([len(cross)])
        there = box(cb, 0, high, k * NB, NB)
        cross.append((0, box(child, 0, high, k * NB, NB), there, there))
        if k >= 3:
            there = box(cb, HALF, NB * (k - 2), k * NB, NB)
            cross_col[k].append(len(cross))
            cross.append((1, box(child, 0, NB * (k - 2), k * NB, NB), there, there))
        else:
            square(0, min(NB * (k + 1), QUARTER), k)
            if k > 0:
                square(1, NB * (k + 1) - QUARTER, k)
    first = len(cross)
    for c in range(2):
        cross.append((c, fl, slot(flg, 2 * par + c, 256), slot(flg, 2 * (1 - par) + c, 256)))
    for c in range(2):
        cross.append((c, fr, slot(frg, 2 * par + c, 256), slot(frg, 2 * (1 - par) + c, 256)))
    cross.append((0, op.at[:, pl.ds(0, NB)], slot(opg, par, NB), slot(opg, 1 - par, NB)))
    cross_fl, cross_rest = (first, first + 1), (first + 2, first + 3, first + 4)

    def local(n):
        return pltpu.make_async_copy(own[n][1], own[n][2], loc.at[n])

    def to_sibling(n):
        return pltpu.make_async_remote_copy(own[n][1], own[n][2], sib_send.at[n], sib_recv.at[n],
                                            device_id=sibling, device_id_type=MESH)

    def to_peer(n):
        return pltpu.make_async_remote_copy(cross[n][1], cross[n][2], x_send.at[n], x_recv.at[n],
                                            device_id=xpeer, device_id_type=MESH)

    def relay(n):
        return pltpu.make_async_remote_copy(cross[n][3], cross[n][3], relay_send.at[n], x_recv.at[n],
                                            device_id=sibling, device_id_type=MESH)

    def start_own(*items):
        for n in items:
            @pl.when(core == own[n][0])
            def _():
                local(n).start()
                to_sibling(n).start()

    def wait_own(*items):
        for n in items:
            @pl.when(core == own[n][0])
            def _():
                local(n).wait()

            @pl.when(core != own[n][0])
            def _():
                to_sibling(n).wait_recv()

    def start_cross(*items):
        for n in items:
            @pl.when(core == cross[n][0])
            def _():
                to_peer(n).start()

    def pass_on(*items):
        for n in items:
            @pl.when(core == cross[n][0])
            def _():
                relay(n).wait_recv()
                relay(n).start()

    def take(*items):
        for n in items:
            @pl.when(core != cross[n][0])
            def _():
                relay(n).wait_recv()

    start_cross(*cross_col[0])
    start_own(0, *own_col[0])
    for k in range(STEPS):
        lf[pl.ds(k * NB, NB), :] = jnp.zeros((NB, N), F32)
    pass_on(*cross_col[0])
    start_cross(*cross_col[1])
    start_own(1, 2, 3)
    for k in range(1, STEPS):
        start_own(*own_col[k])

    def assemble(k):
        buf = k % 2
        right = slice(k * NB, (k + 1) * NB)

        def fill(lo, hi, piece):
            for i in range(lo, hi):
                part = slice(i * NB, (i + 1) * NB)
                both = ca[part, right].astype(F32) + cb[part, right].astype(F32)
                acol[buf, part, :] = both + piece(i)

        def lower(ref, i, j):
            return ref[i * NB : (i + 1) * NB, j * NB : (j + 1) * NB].astype(F32)

        @pl.when(par == 0)
        def _():
            fill(0, min(k + 1, 3), lambda i: lower(og, i, k))
            fill(3, k + 1, lambda i: lower(ox, i - 3, k - 3))

        @pl.when(par == 1)
        def _():
            if k < 3:
                fill(0, k + 1, lambda i: lower(ox, i, k))
            else:
                fill(0, 3, lambda i: lower(og, k - 3, i).T)
                fill(3, k + 1, lambda i: lower(og, i - 3, k))

    def updated(k, i):
        part = slice(i * NB, (i + 1) * NB)
        if i == 0:
            return acol[k % 2, part, :]
        done = slice(0, i * NB)
        return acol[k % 2, part, :] - dot3(lh[part, done], ll[part, done], uh[k % 2, done, :], ul[k % 2, done, :])

    def eliminate(k, i):
        rows = slice(k * NB, (k + 1) * NB)
        part = slice(i * NB, (i + 1) * NB)
        bh, bl = split(updated(k, i))
        u = dot3(xh[part, :], xl[part, :], bh, bl)
        uhi, ulo = split(u)
        uh[k % 2, part, :] = uhi
        ul[k % 2, part, :] = ulo
        t = u.T
        lf[rows, part] = t
        thi, tlo = split(t)
        lh[rows, part] = thi
        ll[rows, part] = tlo

    def ready(k):
        wait_own(*own_col[k])
        wait_own(*{0: (0,), 1: (1, 2, 3)}.get(k, ()))
        take(*cross_col[k])
        assemble(k)

    AHEAD = 2
    writes = []
    for k in range(STEPS):
        rows = slice(k * NB, (k + 1) * NB)
        if k <= AHEAD:
            ready(k)
        if k == 0:
            start_cross(*cross_col[2])
        if k == 1:
            start_cross(*cross_col[4])
        if k == 2:
            start_cross(*cross_fl)
            start_own(*own_fac)
        if k == 3:
            start_cross(*cross_rest)
        if AHEAD <= k < STEPS - 1:
            pass_on(*cross_col[k + 1])

        for i in range(k - 1 if k > AHEAD else 0, k):
            eliminate(k, i)
        diag = updated(k, k)
        acol[k % 2, rows, :] = diag
        r_ref[...] = diag[:H, :H]
        w_ref[...] = eye()
        if k > 0:
            for ref, dst in ((lh, lh_out), (ll, ll_out)):
                copy = pltpu.make_async_copy(
                    box(ref, rows.start, NB, 0, k * NB),
                    box(dst, rows.start, NB, 0, k * NB),
                    out_sem.at[len(writes)],
                )
                copy.start()
                writes.append(copy)
        factor_128(r_ref, w_ref, u_a, x_a, held)
        if k == 0:
            start_cross(*cross_col[3])
        if k == 1:
            start_cross(*cross_col[5])
        if k < AHEAD:
            pass_on(*cross_col[k + 1])
        if k == STEPS - 1:
            pass_on(*cross_fl)
        if AHEAD <= k < STEPS - 1:
            ready(k + 1)
        mid = rows.start + H
        xa = x_a[...]
        uab = dot_split(xa, acol[k % 2, rows.start : mid, H:NB])
        lba = uab.T
        r_ref[...] = acol[k % 2, mid : rows.stop, H:NB] - dot_split(lba, uab)
        w_ref[...] = eye()
        below_a = dot_split(lba, xa)
        if AHEAD <= k < STEPS - 1:
            for i in range(k):
                eliminate(k + 1, i)
        factor_128(r_ref, w_ref, u_b, x_b, held)
        if k == STEPS - 1:
            pass_on(*cross_rest)
        xf[0:H, 0:H] = xa
        xf[0:H, H:NB] = jnp.zeros((H, H), F32)
        xf[H:NB, 0:H] = -dot_split(x_b[...], below_a)
        xf[H:NB, H:NB] = x_b[...]
        lf[rows.start : mid, rows.start : mid] = u_a[...].T
        lf[mid : rows.stop, rows.start : mid] = lba
        lf[mid : rows.stop, mid : rows.stop] = u_b[...].T
        hi, lo = split(xf[...])
        xh[rows, :] = hi
        xl[rows, :] = lo

    mine = pl.ds(pl.multiple_of(par * HALF + core * QUARTER, 128), QUARTER)
    write = pltpu.make_async_copy(lf.at[mine, :], out_lead, out_sem.at[len(writes)])
    write.start()
    writes.append(write)
    wait_own(*own_fac)
    take(*cross_fl, *cross_rest)
    for n in range(len(own)):
        @pl.when(core == own[n][0])
        def _():
            to_sibling(n).wait_send()
    for n in range(len(cross)):
        @pl.when(core == cross[n][0])
        def _():
            to_peer(n).wait_send()
            relay(n).wait_send()
    for copy in writes:
        copy.wait()


def factor_call(child, orig, fl, fr, op):
    any_spec = pl.BlockSpec(memory_space=pl.ANY)
    vmem = pl.BlockSpec(memory_space=pltpu.VMEM)
    dma = pltpu.SemaphoreType.DMA
    return pl.pallas_call(
        factor_kernel,
        out_shape=(
            jax.ShapeDtypeStruct((QUARTER, N), F32),
            jax.ShapeDtypeStruct((N, N), BF16),
            jax.ShapeDtypeStruct((N, N), BF16),
            jax.ShapeDtypeStruct((N, NB), BF16),
            jax.ShapeDtypeStruct((N, NB), BF16),
            jax.ShapeDtypeStruct((N, 1024), BF16),
            jax.ShapeDtypeStruct((NB, 1024), BF16),
            jax.ShapeDtypeStruct((N, 512), BF16),
        ),
        in_specs=[any_spec] * 5,
        out_specs=(any_spec, any_spec, any_spec, vmem, vmem, any_spec, any_spec, any_spec),
        scratch_shapes=[
            pltpu.VMEM((N, N), BF16),
            pltpu.VMEM((N, N), BF16),
            pltpu.VMEM((HALF, N), BF16),
            pltpu.VMEM((HALF, HALF), BF16),
            pltpu.VMEM((2, N, NB), F32),
            pltpu.VMEM((N, N), F32),
            pltpu.VMEM((N, N), BF16),
            pltpu.VMEM((N, N), BF16),
            pltpu.VMEM((2, N, NB), BF16),
            pltpu.VMEM((2, N, NB), BF16),
            pltpu.VMEM((NB, NB), F32),
        ]
        + [pltpu.VMEM((H, H), F32)] * 6
        + [pltpu.VMEM((W * W, H), F32)]
        + [dma((18,)), dma((18,)), dma((18,)), dma((19,)), dma((19,)), dma((19,)), dma((11,))],
        compiler_params=pltpu.CompilerParams(
            collective_id=0, has_side_effects=True, vmem_limit_bytes=56 << 20
        ),
        name="factor",
    )(child, orig, fl, fr, op)


def solve_kernel(
    place, lh_in, ll_in, fl_in, op_in, panel_in, onext_in, xh, xl, fr, mask, upper_out, below_out,
    lh, ll, fl, op, panel, onext, rh, wt, upper, below, sems, next_sem, out_sem,
):
    lead, width = op.shape[1], panel.shape[1]
    tile = 512
    total = lead + width

    def loads(k):
        rows = pl.ds(k * NB, NB)
        pairs = [(fl_in.at[rows, :], fl.at[rows, :]), (op_in.at[rows, :], op.at[rows, :]),
                 (panel_in.at[rows, :], panel.at[rows, :])]
        if k > 0:
            done = pl.ds(0, k * NB)
            pairs += [(lh_in.at[rows, done], lh.at[rows, done]), (ll_in.at[rows, done], ll.at[rows, done])]
        return [pltpu.make_async_copy(src, dst, sems.at[k, n]) for n, (src, dst) in enumerate(pairs)]

    for k in range(STEPS):
        for copy in loads(k):
            copy.start()
    next_load = pltpu.make_async_copy(onext_in, onext, next_sem)
    next_load.start()

    spots, rights = [], []
    for o in range(total // NB):
        spot = [pl.ds(pl.multiple_of(place[2 * o + c] * H, H), H) for c in range(2)]
        spots.append(spot)
        rights.append(jnp.concatenate([fr[:, s] * mask[o : o + 1, c * H : c * H + H] for c, s in enumerate(spot)], axis=1))

    writes = []
    for k in range(STEPS):
        rows = slice(k * NB, (k + 1) * NB)
        for copy in loads(k):
            copy.wait()
        for t in range(total // tile):
            right = slice(t * tile, (t + 1) * tile)
            spread = jnp.concatenate(
                [
                    lax.dot_general(
                        jnp.concatenate([fl[rows, s] for s in spots[o]], axis=1),
                        rights[o],
                        (((1,), (1,)), ((), ())),
                        preferred_element_type=F32,
                    )
                    for o in range(t * tile // NB, (t + 1) * tile // NB)
                ],
                axis=1,
            )
            mine = slice(right.start - lead, right.stop - lead)
            acc = (op[rows, right] if t == 0 else panel[rows, mine]).astype(F32) + spread
            if k > 0:
                done = slice(0, k * NB)
                acc = acc - (dot(lh[rows, done], rh[done, right]) + dot(ll[rows, done], rh[done, right]))
            bh, bl = split(acc)
            u = dot3(xh[rows, :], xl[rows, :], bh, bl)
            rh[rows, right] = u.astype(BF16)
            if t == 0:
                wt[:, rows] = u.T.astype(BF16)
            else:
                upper[rows, mine] = u
        copy = pltpu.make_async_copy(upper.at[pl.ds(k * NB, NB), :], upper_out.at[pl.ds(k * NB, NB), :], out_sem.at[len(writes)])
        copy.start()
        writes.append(copy)

    next_load.wait()
    for t in range(width // NB):
        right = slice(t * NB, (t + 1) * NB)
        below[:, right] = onext[:, right].astype(F32) - dot(wt[...], rh[:, lead + t * NB : lead + (t + 1) * NB])
        copy = pltpu.make_async_copy(below.at[:, pl.ds(t * NB, NB)], below_out.at[:, pl.ds(t * NB, NB)], out_sem.at[len(writes)])
        copy.start()
        writes.append(copy)
    for copy in writes:
        copy.wait()


def solve_call(place, lh, ll, xh, xl, fl, fr, op, panel, mask, onext):
    any_spec = pl.BlockSpec(memory_space=pl.ANY)
    vmem = pl.BlockSpec(memory_space=pltpu.VMEM)
    dma = pltpu.SemaphoreType.DMA
    width = panel.shape[1]
    return pl.pallas_call(
        solve_kernel,
        out_shape=(
            jax.ShapeDtypeStruct(panel.shape, F32),
            jax.ShapeDtypeStruct(onext.shape, F32),
        ),
        in_specs=[pl.BlockSpec(memory_space=pltpu.SMEM)] + [any_spec] * 6 + [vmem] * 4,
        out_specs=(any_spec, any_spec),
        scratch_shapes=[
            pltpu.VMEM((N, N), BF16),
            pltpu.VMEM((N, N), BF16),
            pltpu.VMEM(fl.shape, BF16),
            pltpu.VMEM(op.shape, BF16),
            pltpu.VMEM(panel.shape, BF16),
            pltpu.VMEM(onext.shape, BF16),
            pltpu.VMEM((N, op.shape[1] + width), BF16),
            pltpu.VMEM((op.shape[1], N), BF16),
            pltpu.VMEM(panel.shape, F32),
            pltpu.VMEM(onext.shape, F32),
            dma((STEPS, 5)),
            dma(()),
            dma((STEPS + width // NB,)),
        ],
        compiler_params=pltpu.CompilerParams(vmem_limit_bytes=56 << 20),
        name="solve",
    )(place, lh, ll, fl, op, panel, onext, xh, xl, fr, mask)


def shards(fac_left, fac_right, block_rank, col_map, child_lead, orig_lead, orig_panel, orig_next):
    leaf, core = lax.axis_index("leaf"), lax.axis_index("front")
    par = leaf % 2
    out_lead, lh, ll, xh, xl, flg, frg, opg = factor_call(
        child_lead[0], orig_lead[0], fac_left[0], fac_right[0], orig_panel[0]
    )
    own = par * 8 + core * 4 + jnp.arange(4, dtype=jnp.int32)
    targets = jnp.concatenate([jnp.array([0, 8], jnp.int32), own])
    maps = lax.dynamic_slice_in_dim(col_map, leaf - par, 2, 0).reshape(16)
    ranks = lax.dynamic_slice_in_dim(block_rank, leaf - par, 2, 0).reshape(16)
    hit = (targets[:, None] == maps[None, :]).reshape(6, 2, 8)
    pair = jnp.sum(jnp.where(hit, jnp.arange(8, dtype=jnp.int32) // 2, 0), axis=2)
    place = (pair + jnp.array([[0, 4]], jnp.int32)).reshape(12)
    live = (jnp.arange(RMAX)[None, :] < ranks[:, None]).reshape(1, 2, 8, RMAX)
    used = (hit[..., None] & live).reshape(6, 2, 4, 2 * RMAX)
    mask = jnp.any(used, axis=2).astype(BF16).reshape(6, 4 * RMAX)
    upper, below = solve_call(place, lh, ll, xh, xl, flg, frg, opg, orig_panel[0], mask, orig_next[0])
    return (out_lead[None], upper[None], below[None])


def solution(mesh):
    placed = (
        P("leaf", None, "front"),
        P("leaf", None, "front"),
        P(),
        P(),
        P("leaf", "front", None),
        P("leaf", "front", None),
        P("leaf", None, "front"),
        P("leaf", None, "front"),
    )
    return jax.shard_map(
        shards,
        mesh=mesh,
        in_specs=placed,
        out_specs=(P("leaf", "front", None), P("leaf", None, "front"), P("leaf", None, "front")),
        check_vma=False,
    )
```

```python
import functools

import jax
import jax.numpy as jnp
from jax import lax
from jax.experimental import pallas as pl
from jax.experimental.pallas import tpu as pltpu
from jax.sharding import PartitionSpec as P

MESH = pl.DeviceIdType.MESH
F32 = jnp.float32
BF16 = jnp.bfloat16
N = 1536
NB = 256
H = 128
STEPS = N // NB
HALF = N // 2
QUARTER = N // 4
RMAX = 64
W = 32


def split(x):
    hi = x.astype(BF16)
    return hi, (x - hi.astype(F32)).astype(BF16)


def dot(a, b):
    return jnp.dot(a, b, preferred_element_type=F32)


def dot3(ah, al, bh, bl):
    return dot(ah, bh) + (dot(ah, bl) + dot(al, bh))


def dot_split(a, b):
    return dot3(*split(a), *split(b))


def factor_128(r_ref, x_ref, u_out, x_out, held):
    sub = lax.broadcasted_iota(jnp.int32, (W, H), 0)

    def panel(p, carry):
        top, xtop = r_ref[0:W, :], x_ref[0:W, :]
        col = [jnp.broadcast_to(top[k // 8 * 8 :, k : k + 1], (W - k // 8 * 8, H)) for k in range(W)]
        pivots = jnp.ones((W, H), F32)
        inverses = jnp.ones((W, H), F32)
        for i in range(W):
            base = i // 8 * 8
            held[i * W + base : (i + 1) * W, :] = col[i]
            pivot = col[i][i - base : i - base + 1, :]
            inv = 1.0 / pivot
            m = jnp.where(sub[base:] > i, col[i] * inv, 0.0)
            pivots = jnp.where(sub == i, pivot, pivots)
            inverses = jnp.where(sub == i, inv, inverses)
            for k in range(i + 1, W):
                low = k // 8 * 8
                near = col[i][k - base : k - base + 1, :] if k == i + 1 else held[i * W + k : i * W + k + 1, :]
                col[k] = col[k] - m[low - base :] * near
            row, xrow = top[i : i + 1, :], xtop[i : i + 1, :]
            ntop, nxtop = top[base:] - m * row, xtop[base:] - m * xrow
            top = ntop if base == 0 else jnp.concatenate([top[:base], ntop], axis=0)
            xtop = nxtop if base == 0 else jnp.concatenate([xtop[:base], nxtop], axis=0)
        scale = lax.rsqrt(pivots)
        rows = pl.ds(pl.multiple_of(p * W, W), W)
        u_out[rows, :] = pltpu.roll(top * scale, p * W, 1)
        x_out[rows, :] = xtop * scale
        th, tl = split(top)
        vh, vl = split(jnp.concatenate([top * inverses, xtop * inverses], axis=1))
        update = lax.dot_general(
            jnp.concatenate([th, th, tl], axis=0),
            jnp.concatenate([vh, vl, vh], axis=0),
            (((0,), (0,)), ((), ())),
            preferred_element_type=F32,
        )
        r_ref[0 : H - W, :] = pltpu.roll(r_ref[W:H, :] - update[W:, :H], H - W, 1)
        r_ref[H - W : H, :] = jnp.zeros((W, H), F32)
        x_ref[0 : H - W, :] = x_ref[W:H, :] - update[W:, H:]
        x_ref[H - W : H, :] = jnp.zeros((W, H), F32)
        return carry

    lax.fori_loop(0, H // W, panel, 0)
    low = lax.broadcasted_iota(jnp.int32, (H, H), 0)
    right = lax.broadcasted_iota(jnp.int32, (H, H), 1)
    u_out[...] = jnp.where(right >= low, u_out[...], 0.0)


def eye():
    low = lax.broadcasted_iota(jnp.int32, (H, H), 0)
    col = lax.broadcasted_iota(jnp.int32, (H, H), 1)
    return jnp.where(col == low, 1.0, 0.0).astype(F32)


def factor_kernel(
    child, orig, fl, fr, op,
    out_lead, lh_out, ll_out, xh, xl, fl_out, fr_out, op_out,
    ca, cb, og, ox, acol, lf, lh, ll, uh, ul, xf, r_ref, w_ref, u_a, x_a, u_b, x_b, held, flg, frg, opg,
    loc, sib_send, sib_recv, x_send, relay_send, x_recv, out_sem,
):
    leaf, core = lax.axis_index("leaf"), lax.axis_index("front")
    par = lax.rem(leaf, 2)
    sibling = (leaf, 1 - core)
    xpeer = (leaf + 1 - 2 * par, core)
    barrier = pltpu.get_barrier_semaphore()
    for other in (sibling, xpeer):
        pl.semaphore_signal(barrier, inc=1, device_id=other, device_id_type=MESH)
    pl.semaphore_wait(barrier, 2)

    def slot(ref, index, width):
        return ref.at[:, pl.ds(pl.multiple_of(index * width, 128), width)]

    def box(ref, row, height, col, width):
        return ref.at[pl.ds(row, height), pl.ds(col, width)]

    own = [
        (0, box(orig, 0, NB, 0, NB), box(og, 0, NB, 0, NB)),
        (0, box(orig, 0, NB, NB, N - NB), box(og, 0, NB, NB, N - NB)),
        (0, box(orig, NB, H, 0, N), box(og, NB, H, 0, N)),
        (1, orig, box(og, QUARTER, QUARTER, 0, N)),
    ]
    own_col, cross_col, cross = [], [], []
    for k in range(STEPS):
        own_col.append([len(own)])
        own.append((k // 3, box(child, k % 3 * NB, NB, k * NB, N - k * NB), box(ca, k * NB, NB, k * NB, N - k * NB)))
    own_fac = tuple(range(len(own), len(own) + 5))
    for c in range(2):
        own.append((c, fl, slot(flg, 2 * par + c, 256)))
    for c in range(2):
        own.append((c, fr, slot(frg, 2 * par + c, 256)))
    own.append((0, op.at[:, pl.ds(0, NB)], slot(opg, par, NB)))

    def square(c, height, k):
        src = box(orig, 0, height, pl.multiple_of(par * HALF + k * NB, 128), NB)
        there = box(ox, c * QUARTER, height, k * NB, NB)
        cross_col[k].append(len(cross))
        cross.append((c, src, there, there))

    for k in range(STEPS):
        high = min(NB * (k + 1), HALF)
        cross_col.append([len(cross)])
        there = box(cb, 0, high, k * NB, NB)
        cross.append((0, box(child, 0, high, k * NB, NB), there, there))
        if k >= 3:
            there = box(cb, HALF, NB * (k - 2), k * NB, NB)
            cross_col[k].append(len(cross))
            cross.append((1, box(child, 0, NB * (k - 2), k * NB, NB), there, there))
        else:
            square(0, min(NB * (k + 1), QUARTER), k)
            if k > 0:
                square(1, NB * (k + 1) - QUARTER, k)
    first = len(cross)
    for c in range(2):
        cross.append((c, fl, slot(flg, 2 * par + c, 256), slot(flg, 2 * (1 - par) + c, 256)))
    for c in range(2):
        cross.append((c, fr, slot(frg, 2 * par + c, 256), slot(frg, 2 * (1 - par) + c, 256)))
    cross.append((0, op.at[:, pl.ds(0, NB)], slot(opg, par, NB), slot(opg, 1 - par, NB)))
    cross_fl, cross_rest = (first, first + 1), (first + 2, first + 3, first + 4)

    def local(n):
        return pltpu.make_async_copy(own[n][1], own[n][2], loc.at[n])

    def to_sibling(n):
        return pltpu.make_async_remote_copy(own[n][1], own[n][2], sib_send.at[n], sib_recv.at[n],
                                            device_id=sibling, device_id_type=MESH)

    def to_peer(n):
        return pltpu.make_async_remote_copy(cross[n][1], cross[n][2], x_send.at[n], x_recv.at[n],
                                            device_id=xpeer, device_id_type=MESH)

    def relay(n):
        return pltpu.make_async_remote_copy(cross[n][3], cross[n][3], relay_send.at[n], x_recv.at[n],
                                            device_id=sibling, device_id_type=MESH)

    def start_own(*items):
        for n in items:
            @pl.when(core == own[n][0])
            def _():
                local(n).start()
                to_sibling(n).start()

    def wait_own(*items):
        for n in items:
            @pl.when(core == own[n][0])
            def _():
                local(n).wait()

            @pl.when(core != own[n][0])
            def _():
                to_sibling(n).wait_recv()

    def start_cross(*items):
        for n in items:
            @pl.when(core == cross[n][0])
            def _():
                to_peer(n).start()

    def pass_on(*items):
        for n in items:
            @pl.when(core == cross[n][0])
            def _():
                relay(n).wait_recv()
                relay(n).start()

    def take(*items):
        for n in items:
            @pl.when(core != cross[n][0])
            def _():
                relay(n).wait_recv()

    start_cross(*cross_col[0])
    start_own(0, *own_col[0])
    for k in range(STEPS):
        lf[pl.ds(k * NB, NB), :] = jnp.zeros((NB, N), F32)
    pass_on(*cross_col[0])
    start_cross(*cross_col[1])
    start_own(1, 2, 3)
    for k in range(1, STEPS):
        start_own(*own_col[k])

    def assemble(k):
        buf = k % 2
        right = slice(k * NB, (k + 1) * NB)

        def fill(lo, hi, piece):
            for i in range(lo, hi):
                part = slice(i * NB, (i + 1) * NB)
                both = ca[part, right].astype(F32) + cb[part, right].astype(F32)
                acol[buf, part, :] = both + piece(i)

        def lower(ref, i, j):
            return ref[i * NB : (i + 1) * NB, j * NB : (j + 1) * NB].astype(F32)

        @pl.when(par == 0)
        def _():
            fill(0, min(k + 1, 3), lambda i: lower(og, i, k))
            fill(3, k + 1, lambda i: lower(ox, i - 3, k - 3))

        @pl.when(par == 1)
        def _():
            if k < 3:
                fill(0, k + 1, lambda i: lower(ox, i, k))
            else:
                fill(0, 3, lambda i: lower(og, k - 3, i).T)
                fill(3, k + 1, lambda i: lower(og, i - 3, k))

    def updated(k, i):
        part = slice(i * NB, (i + 1) * NB)
        if i == 0:
            return acol[k % 2, part, :]
        done = slice(0, i * NB)
        return acol[k % 2, part, :] - dot3(lh[part, done], ll[part, done], uh[k % 2, done, :], ul[k % 2, done, :])

    def eliminate(k, i):
        rows = slice(k * NB, (k + 1) * NB)
        part = slice(i * NB, (i + 1) * NB)
        bh, bl = split(updated(k, i))
        u = dot3(xh[part, :], xl[part, :], bh, bl)
        uhi, ulo = split(u)
        uh[k % 2, part, :] = uhi
        ul[k % 2, part, :] = ulo
        t = u.T
        lf[rows, part] = t
        thi, tlo = split(t)
        lh[rows, part] = thi
        ll[rows, part] = tlo

    def ready(k):
        wait_own(*own_col[k])
        wait_own(*{0: (0,), 1: (1, 2, 3)}.get(k, ()))
        take(*cross_col[k])
        assemble(k)

    AHEAD = 2
    writes = []

    def hand_over(half):
        for ref, dst, width in ((flg, fl_out, 512), (frg, fr_out, 512), (opg, op_out, NB)):
            copy = pltpu.make_async_copy(slot(ref, half, width), slot(dst, half, width), out_sem.at[len(writes)])
            copy.start()
            writes.append(copy)

    for k in range(STEPS):
        rows = slice(k * NB, (k + 1) * NB)
        if k <= AHEAD:
            ready(k)
        if k == 2:
            start_own(*own_fac)
        if k == 3:
            start_cross(*cross_rest)
        if k == 4:
            wait_own(*own_fac)
            hand_over(par)
        if AHEAD <= k < STEPS - 1:
            pass_on(*cross_col[k + 1])

        for i in range(k - 1 if k > AHEAD else 0, k):
            eliminate(k, i)
        diag = updated(k, k)
        acol[k % 2, rows, :] = diag
        r_ref[...] = diag[:H, :H]
        w_ref[...] = eye()
        if k > 0:
            for ref, dst in ((lh, lh_out), (ll, ll_out)):
                copy = pltpu.make_async_copy(
                    box(ref, rows.start, NB, 0, k * NB),
                    box(dst, rows.start, NB, 0, k * NB),
                    out_sem.at[len(writes)],
                )
                copy.start()
                writes.append(copy)
        factor_128(r_ref, w_ref, u_a, x_a, held)
        if k == 0:
            start_cross(*cross_col[2])
        if k == 1:
            start_cross(*cross_col[4])
        if k == 2:
            start_cross(*cross_fl)
        if AHEAD <= k < STEPS - 1:
            ready(k + 1)
        mid = rows.start + H
        xa = x_a[...]
        uab = dot_split(xa, acol[k % 2, rows.start : mid, H:NB])
        lba = uab.T
        r_ref[...] = acol[k % 2, mid : rows.stop, H:NB] - dot_split(lba, uab)
        w_ref[...] = eye()
        below_a = dot_split(lba, xa)
        if AHEAD <= k < STEPS - 1:
            for i in range(k):
                eliminate(k + 1, i)
        factor_128(r_ref, w_ref, u_b, x_b, held)
        if k < AHEAD:
            pass_on(*cross_col[k + 1])
            start_cross(*cross_col[3 + 2 * k])
        if k == STEPS - 1:
            pass_on(*cross_fl, *cross_rest)
        xf[0:H, 0:H] = xa
        xf[0:H, H:NB] = jnp.zeros((H, H), F32)
        xf[H:NB, 0:H] = -dot_split(x_b[...], below_a)
        xf[H:NB, H:NB] = x_b[...]
        lf[rows.start : mid, rows.start : mid] = u_a[...].T
        lf[mid : rows.stop, rows.start : mid] = lba
        lf[mid : rows.stop, mid : rows.stop] = u_b[...].T
        hi, lo = split(xf[...])
        xh[rows, :] = hi
        xl[rows, :] = lo

    mine = pl.ds(pl.multiple_of(par * HALF + core * QUARTER, 128), QUARTER)
    write = pltpu.make_async_copy(lf.at[mine, :], out_lead, out_sem.at[len(writes)])
    write.start()
    writes.append(write)
    take(*cross_fl, *cross_rest)
    hand_over(1 - par)
    for n in range(len(own)):
        @pl.when(core == own[n][0])
        def _():
            to_sibling(n).wait_send()
    for n in range(len(cross)):
        @pl.when(core == cross[n][0])
        def _():
            to_peer(n).wait_send()
            relay(n).wait_send()
    for copy in writes:
        copy.wait()


def factor_call(child, orig, fl, fr, op):
    any_spec = pl.BlockSpec(memory_space=pl.ANY)
    vmem = pl.BlockSpec(memory_space=pltpu.VMEM)
    dma = pltpu.SemaphoreType.DMA
    return pl.pallas_call(
        factor_kernel,
        out_shape=(
            jax.ShapeDtypeStruct((QUARTER, N), F32),
            jax.ShapeDtypeStruct((N, N), BF16),
            jax.ShapeDtypeStruct((N, N), BF16),
            jax.ShapeDtypeStruct((N, NB), BF16),
            jax.ShapeDtypeStruct((N, NB), BF16),
            jax.ShapeDtypeStruct((N, 1024), BF16),
            jax.ShapeDtypeStruct((NB, 1024), BF16),
            jax.ShapeDtypeStruct((N, 512), BF16),
        ),
        in_specs=[any_spec] * 5,
        out_specs=(any_spec, any_spec, any_spec, vmem, vmem, any_spec, any_spec, any_spec),
        scratch_shapes=[
            pltpu.VMEM((N, N), BF16),
            pltpu.VMEM((N, N), BF16),
            pltpu.VMEM((HALF, N), BF16),
            pltpu.VMEM((HALF, HALF), BF16),
            pltpu.VMEM((2, N, NB), F32),
            pltpu.VMEM((N, N), F32),
            pltpu.VMEM((N, N), BF16),
            pltpu.VMEM((N, N), BF16),
            pltpu.VMEM((2, N, NB), BF16),
            pltpu.VMEM((2, N, NB), BF16),
            pltpu.VMEM((NB, NB), F32),
        ]
        + [pltpu.VMEM((H, H), F32)] * 6
        + [pltpu.VMEM((W * W, H), F32)]
        + [pltpu.VMEM((N, 1024), BF16), pltpu.VMEM((NB, 1024), BF16), pltpu.VMEM((N, 512), BF16)]
        + [dma((15,)), dma((15,)), dma((15,)), dma((19,)), dma((19,)), dma((19,)), dma((17,))],
        compiler_params=pltpu.CompilerParams(
            collective_id=0, has_side_effects=True, vmem_limit_bytes=56 << 20
        ),
        name="factor",
    )(child, orig, fl, fr, op)


def solve_kernel(
    place, lh_in, ll_in, fl_in, op_in, panel_in, onext_in, xh, xl, fr, mask, upper_out, below_out,
    lh, ll, fl, op, panel, onext, rh, wt, upper, below, sems, next_sem, out_sem,
):
    lead, width = op.shape[1], panel.shape[1]
    tile = 512
    total = lead + width

    def loads(k):
        rows = pl.ds(k * NB, NB)
        pairs = [(fl_in.at[rows, :], fl.at[rows, :]), (op_in.at[rows, :], op.at[rows, :]),
                 (panel_in.at[rows, :], panel.at[rows, :])]
        if k > 0:
            done = pl.ds(0, k * NB)
            pairs += [(lh_in.at[rows, done], lh.at[rows, done]), (ll_in.at[rows, done], ll.at[rows, done])]
        return [pltpu.make_async_copy(src, dst, sems.at[k, n]) for n, (src, dst) in enumerate(pairs)]

    for k in range(STEPS):
        for copy in loads(k):
            copy.start()
    next_load = pltpu.make_async_copy(onext_in, onext, next_sem)
    next_load.start()

    spots, rights = [], []
    for o in range(total // NB):
        spot = [pl.ds(pl.multiple_of(place[2 * o + c] * H, H), H) for c in range(2)]
        spots.append(spot)
        rights.append(jnp.concatenate([fr[:, s] * mask[o : o + 1, c * H : c * H + H] for c, s in enumerate(spot)], axis=1))

    writes = []
    for k in range(STEPS):
        rows = slice(k * NB, (k + 1) * NB)
        for copy in loads(k):
            copy.wait()
        for t in range(total // tile):
            right = slice(t * tile, (t + 1) * tile)
            spread = jnp.concatenate(
                [
                    lax.dot_general(
                        jnp.concatenate([fl[rows, s] for s in spots[o]], axis=1),
                        rights[o],
                        (((1,), (1,)), ((), ())),
                        preferred_element_type=F32,
                    )
                    for o in range(t * tile // NB, (t + 1) * tile // NB)
                ],
                axis=1,
            )
            mine = slice(right.start - lead, right.stop - lead)
            acc = (op[rows, right] if t == 0 else panel[rows, mine]).astype(F32) + spread
            if k > 0:
                done = slice(0, k * NB)
                acc = acc - (dot(lh[rows, done], rh[done, right]) + dot(ll[rows, done], rh[done, right]))
            bh, bl = split(acc)
            u = dot3(xh[rows, :], xl[rows, :], bh, bl)
            rh[rows, right] = u.astype(BF16)
            if t == 0:
                wt[:, rows] = u.T.astype(BF16)
            else:
                upper[rows, mine] = u
        copy = pltpu.make_async_copy(upper.at[pl.ds(k * NB, NB), :], upper_out.at[pl.ds(k * NB, NB), :], out_sem.at[len(writes)])
        copy.start()
        writes.append(copy)

    next_load.wait()
    for t in range(width // NB):
        right = slice(t * NB, (t + 1) * NB)
        below[:, right] = onext[:, right].astype(F32) - dot(wt[...], rh[:, lead + t * NB : lead + (t + 1) * NB])
        copy = pltpu.make_async_copy(below.at[:, pl.ds(t * NB, NB)], below_out.at[:, pl.ds(t * NB, NB)], out_sem.at[len(writes)])
        copy.start()
        writes.append(copy)
    for copy in writes:
        copy.wait()


def solve_call(place, lh, ll, xh, xl, fl, fr, op, panel, mask, onext):
    any_spec = pl.BlockSpec(memory_space=pl.ANY)
    vmem = pl.BlockSpec(memory_space=pltpu.VMEM)
    dma = pltpu.SemaphoreType.DMA
    width = panel.shape[1]
    return pl.pallas_call(
        solve_kernel,
        out_shape=(
            jax.ShapeDtypeStruct(panel.shape, F32),
            jax.ShapeDtypeStruct(onext.shape, F32),
        ),
        in_specs=[pl.BlockSpec(memory_space=pltpu.SMEM)] + [any_spec] * 6 + [vmem] * 4,
        out_specs=(any_spec, any_spec),
        scratch_shapes=[
            pltpu.VMEM((N, N), BF16),
            pltpu.VMEM((N, N), BF16),
            pltpu.VMEM(fl.shape, BF16),
            pltpu.VMEM(op.shape, BF16),
            pltpu.VMEM(panel.shape, BF16),
            pltpu.VMEM(onext.shape, BF16),
            pltpu.VMEM((N, op.shape[1] + width), BF16),
            pltpu.VMEM((op.shape[1], N), BF16),
            pltpu.VMEM(panel.shape, F32),
            pltpu.VMEM(onext.shape, F32),
            dma((STEPS, 5)),
            dma(()),
            dma((STEPS + width // NB,)),
        ],
        compiler_params=pltpu.CompilerParams(vmem_limit_bytes=56 << 20),
        name="solve",
    )(place, lh, ll, fl, op, panel, onext, xh, xl, fr, mask)


def shards(fac_left, fac_right, block_rank, col_map, child_lead, orig_lead, orig_panel, orig_next):
    leaf, core = lax.axis_index("leaf"), lax.axis_index("front")
    par = leaf % 2
    out_lead, lh, ll, xh, xl, flg, frg, opg = factor_call(
        child_lead[0], orig_lead[0], fac_left[0], fac_right[0], orig_panel[0]
    )
    own = par * 8 + core * 4 + jnp.arange(4, dtype=jnp.int32)
    targets = jnp.concatenate([jnp.array([0, 8], jnp.int32), own])
    maps = lax.dynamic_slice_in_dim(col_map, leaf - par, 2, 0).reshape(16)
    ranks = lax.dynamic_slice_in_dim(block_rank, leaf - par, 2, 0).reshape(16)
    hit = (targets[:, None] == maps[None, :]).reshape(6, 2, 8)
    pair = jnp.sum(jnp.where(hit, jnp.arange(8, dtype=jnp.int32) // 2, 0), axis=2)
    place = (pair + jnp.array([[0, 4]], jnp.int32)).reshape(12)
    live = (jnp.arange(RMAX)[None, :] < ranks[:, None]).reshape(1, 2, 8, RMAX)
    used = (hit[..., None] & live).reshape(6, 2, 4, 2 * RMAX)
    mask = jnp.any(used, axis=2).astype(BF16).reshape(6, 4 * RMAX)
    upper, below = solve_call(place, lh, ll, xh, xl, flg, frg, opg, orig_panel[0], mask, orig_next[0])
    return (out_lead[None], upper[None], below[None])


def solution(mesh):
    placed = (
        P("leaf", None, "front"),
        P("leaf", None, "front"),
        P(),
        P(),
        P("leaf", "front", None),
        P("leaf", "front", None),
        P("leaf", None, "front"),
        P("leaf", None, "front"),
    )
    return jax.shard_map(
        shards,
        mesh=mesh,
        in_specs=placed,
        out_specs=(P("leaf", "front", None), P("leaf", None, "front"), P("leaf", None, "front")),
        check_vma=False,
    )
```

```python
import functools

import jax
import jax.numpy as jnp
from jax import lax
from jax.experimental import pallas as pl
from jax.experimental.pallas import tpu as pltpu
from jax.sharding import PartitionSpec as P

MESH = pl.DeviceIdType.MESH
F32 = jnp.float32
BF16 = jnp.bfloat16
N = 1536
NB = 256
H = 128
STEPS = N // NB
HALF = N // 2
QUARTER = N // 4
RMAX = 64
W = 32


def split(x):
    hi = x.astype(BF16)
    return hi, (x - hi.astype(F32)).astype(BF16)


def dot(a, b):
    return jnp.dot(a, b, preferred_element_type=F32)


def dot3(ah, al, bh, bl):
    return dot(ah, bh) + (dot(ah, bl) + dot(al, bh))


def dot_split(a, b):
    return dot3(*split(a), *split(b))


def factor_128(r_ref, x_ref, u_out, x_out, held):
    sub = lax.broadcasted_iota(jnp.int32, (W, H), 0)

    def panel(p, carry):
        top, xtop = r_ref[0:W, :], x_ref[0:W, :]
        col = [jnp.broadcast_to(top[k // 8 * 8 :, k : k + 1], (W - k // 8 * 8, H)) for k in range(W)]
        pivots = jnp.ones((W, H), F32)
        inverses = jnp.ones((W, H), F32)
        for i in range(W):
            base = i // 8 * 8
            held[i * W + base : (i + 1) * W, :] = col[i]
            pivot = col[i][i - base : i - base + 1, :]
            inv = 1.0 / pivot
            m = jnp.where(sub[base:] > i, col[i] * inv, 0.0)
            pivots = jnp.where(sub == i, pivot, pivots)
            inverses = jnp.where(sub == i, inv, inverses)
            for k in range(i + 1, W):
                low = k // 8 * 8
                near = col[i][k - base : k - base + 1, :] if k == i + 1 else held[i * W + k : i * W + k + 1, :]
                col[k] = col[k] - m[low - base :] * near
            row, xrow = top[i : i + 1, :], xtop[i : i + 1, :]
            ntop, nxtop = top[base:] - m * row, xtop[base:] - m * xrow
            top = ntop if base == 0 else jnp.concatenate([top[:base], ntop], axis=0)
            xtop = nxtop if base == 0 else jnp.concatenate([xtop[:base], nxtop], axis=0)
        scale = lax.rsqrt(pivots)
        rows = pl.ds(pl.multiple_of(p * W, W), W)
        u_out[rows, :] = pltpu.roll(top * scale, p * W, 1)
        x_out[rows, :] = xtop * scale
        th, tl = split(top)
        vh, vl = split(jnp.concatenate([top * inverses, xtop * inverses], axis=1))
        update = lax.dot_general(
            jnp.concatenate([th, th, tl], axis=0),
            jnp.concatenate([vh, vl, vh], axis=0),
            (((0,), (0,)), ((), ())),
            preferred_element_type=F32,
        )
        r_ref[0 : H - W, :] = pltpu.roll(r_ref[W:H, :] - update[W:, :H], H - W, 1)
        r_ref[H - W : H, :] = jnp.zeros((W, H), F32)
        x_ref[0 : H - W, :] = x_ref[W:H, :] - update[W:, H:]
        x_ref[H - W : H, :] = jnp.zeros((W, H), F32)
        return carry

    lax.fori_loop(0, H // W, panel, 0)
    low = lax.broadcasted_iota(jnp.int32, (H, H), 0)
    right = lax.broadcasted_iota(jnp.int32, (H, H), 1)
    u_out[...] = jnp.where(right >= low, u_out[...], 0.0)


def eye():
    low = lax.broadcasted_iota(jnp.int32, (H, H), 0)
    col = lax.broadcasted_iota(jnp.int32, (H, H), 1)
    return jnp.where(col == low, 1.0, 0.0).astype(F32)


def factor_kernel(
    child, orig, fl, fr, op,
    out_lead, lh_out, ll_out, xh, xl, fl_out, fr_out, op_out,
    ca, cb, og, ox, acol, lf, lh, ll, uh, ul, xf, r_ref, w_ref, u_a, x_a, u_b, x_b, held, flg, frg, opg,
    loc, sib_send, sib_recv, x_send, relay_send, x_recv, out_sem,
):
    leaf, core = lax.axis_index("leaf"), lax.axis_index("front")
    par = lax.rem(leaf, 2)
    sibling = (leaf, 1 - core)
    xpeer = (leaf + 1 - 2 * par, core)
    barrier = pltpu.get_barrier_semaphore()
    for other in (sibling, xpeer):
        pl.semaphore_signal(barrier, inc=1, device_id=other, device_id_type=MESH)
    pl.semaphore_wait(barrier, 2)

    def slot(ref, index, width):
        return ref.at[:, pl.ds(pl.multiple_of(index * width, 128), width)]

    def box(ref, row, height, col, width):
        return ref.at[pl.ds(row, height), pl.ds(col, width)]

    own = [
        (0, box(orig, 0, NB, 0, NB), box(og, 0, NB, 0, NB)),
        (0, box(orig, 0, NB, NB, N - NB), box(og, 0, NB, NB, N - NB)),
        (0, box(orig, NB, H, 0, N), box(og, NB, H, 0, N)),
        (1, orig, box(og, QUARTER, QUARTER, 0, N)),
    ]
    own_col, cross_col, cross = [], [], []
    for k in range(STEPS):
        own_col.append([len(own)])
        own.append((k // 3, box(child, k % 3 * NB, NB, k * NB, N - k * NB), box(ca, k * NB, NB, k * NB, N - k * NB)))
    own_fac = tuple(range(len(own), len(own) + 5))
    for c in range(2):
        own.append((c, fl, slot(flg, 2 * par + c, 256)))
    for c in range(2):
        own.append((c, fr, slot(frg, 2 * par + c, 256)))
    own.append((0, op.at[:, pl.ds(0, NB)], slot(opg, par, NB)))

    def square(c, height, k):
        src = box(orig, 0, height, pl.multiple_of(par * HALF + k * NB, 128), NB)
        there = box(ox, c * QUARTER, height, k * NB, NB)
        cross_col[k].append(len(cross))
        cross.append((c, src, there, there))

    for k in range(STEPS):
        high = min(NB * (k + 1), HALF)
        cross_col.append([len(cross)])
        there = box(cb, 0, high, k * NB, NB)
        cross.append((0, box(child, 0, high, k * NB, NB), there, there))
        if k >= 3:
            there = box(cb, HALF, NB * (k - 2), k * NB, NB)
            cross_col[k].append(len(cross))
            cross.append((1, box(child, 0, NB * (k - 2), k * NB, NB), there, there))
        else:
            square(0, min(NB * (k + 1), QUARTER), k)
            if k > 0:
                square(1, NB * (k + 1) - QUARTER, k)
    first = len(cross)
    for c in range(2):
        cross.append((c, fl, slot(flg, 2 * par + c, 256), slot(flg, 2 * (1 - par) + c, 256)))
    for c in range(2):
        cross.append((c, fr, slot(frg, 2 * par + c, 256), slot(frg, 2 * (1 - par) + c, 256)))
    cross.append((0, op.at[:, pl.ds(0, NB)], slot(opg, par, NB), slot(opg, 1 - par, NB)))
    cross_fl, cross_rest = (first, first + 1), (first + 2, first + 3, first + 4)

    def local(n):
        return pltpu.make_async_copy(own[n][1], own[n][2], loc.at[n])

    def to_sibling(n):
        return pltpu.make_async_remote_copy(own[n][1], own[n][2], sib_send.at[n], sib_recv.at[n],
                                            device_id=sibling, device_id_type=MESH)

    def to_peer(n):
        return pltpu.make_async_remote_copy(cross[n][1], cross[n][2], x_send.at[n], x_recv.at[n],
                                            device_id=xpeer, device_id_type=MESH)

    def relay(n):
        return pltpu.make_async_remote_copy(cross[n][3], cross[n][3], relay_send.at[n], x_recv.at[n],
                                            device_id=sibling, device_id_type=MESH)

    def start_own(*items):
        for n in items:
            @pl.when(core == own[n][0])
            def _():
                local(n).start()
                to_sibling(n).start()

    def wait_own(*items):
        for n in items:
            @pl.when(core == own[n][0])
            def _():
                local(n).wait()

            @pl.when(core != own[n][0])
            def _():
                to_sibling(n).wait_recv()

    def start_cross(*items):
        for n in items:
            @pl.when(core == cross[n][0])
            def _():
                to_peer(n).start()

    def pass_on(*items):
        for n in items:
            @pl.when(core == cross[n][0])
            def _():
                relay(n).wait_recv()
                relay(n).start()

    def take(*items):
        for n in items:
            @pl.when(core != cross[n][0])
            def _():
                relay(n).wait_recv()

    start_cross(*cross_col[0])
    start_own(0, *own_col[0])
    for k in range(STEPS):
        lf[pl.ds(k * NB, NB), :] = jnp.zeros((NB, N), F32)
    pass_on(*cross_col[0])
    start_cross(*cross_col[1])
    start_own(1, 2, 3)
    for k in range(1, STEPS):
        start_own(*own_col[k])

    def assemble(k):
        buf = k % 2
        right = slice(k * NB, (k + 1) * NB)

        def fill(lo, hi, piece):
            for i in range(lo, hi):
                part = slice(i * NB, (i + 1) * NB)
                both = ca[part, right].astype(F32) + cb[part, right].astype(F32)
                acol[buf, part, :] = both + piece(i)

        def lower(ref, i, j):
            return ref[i * NB : (i + 1) * NB, j * NB : (j + 1) * NB].astype(F32)

        @pl.when(par == 0)
        def _():
            fill(0, min(k + 1, 3), lambda i: lower(og, i, k))
            fill(3, k + 1, lambda i: lower(ox, i - 3, k - 3))

        @pl.when(par == 1)
        def _():
            if k < 3:
                fill(0, k + 1, lambda i: lower(ox, i, k))
            else:
                fill(0, 3, lambda i: lower(og, k - 3, i).T)
                fill(3, k + 1, lambda i: lower(og, i - 3, k))

    def updated(k, i):
        part = slice(i * NB, (i + 1) * NB)
        if i == 0:
            return acol[k % 2, part, :]
        done = slice(0, i * NB)
        return acol[k % 2, part, :] - dot3(lh[part, done], ll[part, done], uh[k % 2, done, :], ul[k % 2, done, :])

    def eliminate(k, i):
        rows = slice(k * NB, (k + 1) * NB)
        part = slice(i * NB, (i + 1) * NB)
        bh, bl = split(updated(k, i))
        u = dot3(xh[part, :], xl[part, :], bh, bl)
        uhi, ulo = split(u)
        uh[k % 2, part, :] = uhi
        ul[k % 2, part, :] = ulo
        t = u.T
        lf[rows, part] = t
        thi, tlo = split(t)
        lh[rows, part] = thi
        ll[rows, part] = tlo

    def ready(k):
        wait_own(*own_col[k])
        wait_own(*{0: (0,), 1: (1, 2, 3)}.get(k, ()))
        take(*cross_col[k])
        assemble(k)

    AHEAD = 2
    writes = []

    def hand_over(half):
        for ref, dst, width in ((flg, fl_out, 512), (frg, fr_out, 512), (opg, op_out, NB)):
            copy = pltpu.make_async_copy(slot(ref, half, width), slot(dst, half, width), out_sem.at[len(writes)])
            copy.start()
            writes.append(copy)

    for k in range(STEPS):
        rows = slice(k * NB, (k + 1) * NB)
        if k <= AHEAD:
            ready(k)
        if k == 2:
            start_own(*own_fac)
        if k == 3:
            start_cross(*cross_rest)
        if k == 4:
            wait_own(*own_fac)
            hand_over(par)
        if AHEAD <= k < STEPS - 1:
            pass_on(*cross_col[k + 1])

        for i in range(k - 1 if k > AHEAD else 0, k):
            eliminate(k, i)
        diag = updated(k, k)
        acol[k % 2, rows, :] = diag
        r_ref[...] = diag[:H, :H]
        w_ref[...] = eye()
        if k > 0:
            for ref, dst in ((lh, lh_out), (ll, ll_out)):
                copy = pltpu.make_async_copy(
                    box(ref, rows.start, NB, 0, k * NB),
                    box(dst, rows.start, NB, 0, k * NB),
                    out_sem.at[len(writes)],
                )
                copy.start()
                writes.append(copy)
        factor_128(r_ref, w_ref, u_a, x_a, held)
        if k == 0:
            start_cross(*cross_col[2])
        if k == 1:
            start_cross(*cross_col[4])
        if k == 2:
            start_cross(*cross_fl)
        if AHEAD <= k < STEPS - 1:
            ready(k + 1)
        mid = rows.start + H
        xa = x_a[...]
        uab = dot_split(xa, acol[k % 2, rows.start : mid, H:NB])
        lba = uab.T
        r_ref[...] = acol[k % 2, mid : rows.stop, H:NB] - dot_split(lba, uab)
        w_ref[...] = eye()
        below_a = dot_split(lba, xa)
        if AHEAD <= k < STEPS - 1:
            for i in range(k):
                eliminate(k + 1, i)
        factor_128(r_ref, w_ref, u_b, x_b, held)
        if k < AHEAD:
            pass_on(*cross_col[k + 1])
            start_cross(*cross_col[3 + 2 * k])
        if k == STEPS - 1:
            pass_on(*cross_fl, *cross_rest)
        xf[0:H, 0:H] = xa
        xf[0:H, H:NB] = jnp.zeros((H, H), F32)
        xf[H:NB, 0:H] = -dot_split(x_b[...], below_a)
        xf[H:NB, H:NB] = x_b[...]
        lf[rows.start : mid, rows.start : mid] = u_a[...].T
        lf[mid : rows.stop, rows.start : mid] = lba
        lf[mid : rows.stop, mid : rows.stop] = u_b[...].T
        hi, lo = split(xf[...])
        xh[rows, :] = hi
        xl[rows, :] = lo

    mine = pl.ds(pl.multiple_of(par * HALF + core * QUARTER, 128), QUARTER)
    write = pltpu.make_async_copy(lf.at[mine, :], out_lead, out_sem.at[len(writes)])
    write.start()
    writes.append(write)
    take(*cross_fl, *cross_rest)
    hand_over(1 - par)
    for n in range(len(own)):
        @pl.when(core == own[n][0])
        def _():
            to_sibling(n).wait_send()
    for n in range(len(cross)):
        @pl.when(core == cross[n][0])
        def _():
            to_peer(n).wait_send()
            relay(n).wait_send()
    for copy in writes:
        copy.wait()


def factor_call(child, orig, fl, fr, op):
    any_spec = pl.BlockSpec(memory_space=pl.ANY)
    vmem = pl.BlockSpec(memory_space=pltpu.VMEM)
    dma = pltpu.SemaphoreType.DMA
    return pl.pallas_call(
        factor_kernel,
        out_shape=(
            jax.ShapeDtypeStruct((QUARTER, N), F32),
            jax.ShapeDtypeStruct((N, N), BF16),
            jax.ShapeDtypeStruct((N, N), BF16),
            jax.ShapeDtypeStruct((N, NB), BF16),
            jax.ShapeDtypeStruct((N, NB), BF16),
            jax.ShapeDtypeStruct((N, 1024), BF16),
            jax.ShapeDtypeStruct((NB, 1024), BF16),
            jax.ShapeDtypeStruct((N, 512), BF16),
        ),
        in_specs=[any_spec] * 5,
        out_specs=(any_spec, any_spec, any_spec, vmem, vmem, any_spec, any_spec, any_spec),
        scratch_shapes=[
            pltpu.VMEM((N, N), BF16),
            pltpu.VMEM((N, N), BF16),
            pltpu.VMEM((HALF, N), BF16),
            pltpu.VMEM((HALF, HALF), BF16),
            pltpu.VMEM((2, N, NB), F32),
            pltpu.VMEM((N, N), F32),
            pltpu.VMEM((N, N), BF16),
            pltpu.VMEM((N, N), BF16),
            pltpu.VMEM((2, N, NB), BF16),
            pltpu.VMEM((2, N, NB), BF16),
            pltpu.VMEM((NB, NB), F32),
        ]
        + [pltpu.VMEM((H, H), F32)] * 6
        + [pltpu.VMEM((W * W, H), F32)]
        + [pltpu.VMEM((N, 1024), BF16), pltpu.VMEM((NB, 1024), BF16), pltpu.VMEM((N, 512), BF16)]
        + [dma((15,)), dma((15,)), dma((15,)), dma((19,)), dma((19,)), dma((19,)), dma((17,))],
        compiler_params=pltpu.CompilerParams(
            collective_id=0, has_side_effects=True, vmem_limit_bytes=56 << 20
        ),
        name="factor",
    )(child, orig, fl, fr, op)


def solve_kernel(
    maps, ranks, lh_in, ll_in, fl_in, op_in, panel_in, onext_in, xh, xl, fr, upper_out, below_out,
    lh, ll, fl, op, panel, onext, rh, wt, upper, below, sems, next_sem, out_sem,
):
    lead, width = op.shape[1], panel.shape[1]
    tile = 512
    total = lead + width

    def loads(k):
        rows = pl.ds(k * NB, NB)
        pairs = [(fl_in.at[rows, :], fl.at[rows, :]), (op_in.at[rows, :], op.at[rows, :]),
                 (panel_in.at[rows, :], panel.at[rows, :])]
        if k > 0:
            done = pl.ds(0, k * NB)
            pairs += [(lh_in.at[rows, done], lh.at[rows, done]), (ll_in.at[rows, done], ll.at[rows, done])]
        return [pltpu.make_async_copy(src, dst, sems.at[k, n]) for n, (src, dst) in enumerate(pairs)]

    for k in range(STEPS):
        for copy in loads(k):
            copy.start()
    next_load = pltpu.make_async_copy(onext_in, onext, next_sem)
    next_load.start()

    leaf, core = lax.axis_index("leaf"), lax.axis_index("front")
    par = lax.rem(leaf, 2)
    lane = lax.broadcasted_iota(jnp.int32, (1, H), 1)
    spots, rights = [], []
    for o in range(total // NB):
        target = 8 * o if o < 2 else par * 8 + core * 4 + (o - 2)
        spot, pieces = [], []
        for c in range(2):
            block, rank = jnp.int32(0), jnp.int32(0)
            for n in range(8):
                hit = maps[leaf - par + c, n] == target
                block = jnp.where(hit, n, block)
                rank = jnp.where(hit, ranks[leaf - par + c, n], rank)
            low = lax.rem(block, 2) * RMAX
            used = jnp.where((lane >= low) & (lane < low + rank), 1.0, 0.0).astype(BF16)
            spot.append(pl.ds(pl.multiple_of((4 * c + lax.div(block, 2)) * H, H), H))
            pieces.append(fr[:, spot[c]] * used)
        spots.append(spot)
        rights.append(jnp.concatenate(pieces, axis=1))

    writes = []
    for k in range(STEPS):
        rows = slice(k * NB, (k + 1) * NB)
        for copy in loads(k):
            copy.wait()
        for t in range(total // tile):
            right = slice(t * tile, (t + 1) * tile)
            spread = jnp.concatenate(
                [
                    lax.dot_general(
                        jnp.concatenate([fl[rows, s] for s in spots[o]], axis=1),
                        rights[o],
                        (((1,), (1,)), ((), ())),
                        preferred_element_type=F32,
                    )
                    for o in range(t * tile // NB, (t + 1) * tile // NB)
                ],
                axis=1,
            )
            mine = slice(right.start - lead, right.stop - lead)
            acc = (op[rows, right] if t == 0 else panel[rows, mine]).astype(F32) + spread
            if k > 0:
                done = slice(0, k * NB)
                acc = acc - (dot(lh[rows, done], rh[done, right]) + dot(ll[rows, done], rh[done, right]))
            bh, bl = split(acc)
            u = dot3(xh[rows, :], xl[rows, :], bh, bl)
            rh[rows, right] = u.astype(BF16)
            if t == 0:
                wt[:, rows] = u.T.astype(BF16)
            else:
                upper[rows, mine] = u
        copy = pltpu.make_async_copy(upper.at[pl.ds(k * NB, NB), :], upper_out.at[pl.ds(k * NB, NB), :], out_sem.at[len(writes)])
        copy.start()
        writes.append(copy)

    next_load.wait()
    for t in range(width // NB):
        right = slice(t * NB, (t + 1) * NB)
        below[:, right] = onext[:, right].astype(F32) - dot(wt[...], rh[:, lead + t * NB : lead + (t + 1) * NB])
        copy = pltpu.make_async_copy(below.at[:, pl.ds(t * NB, NB)], below_out.at[:, pl.ds(t * NB, NB)], out_sem.at[len(writes)])
        copy.start()
        writes.append(copy)
    for copy in writes:
        copy.wait()


def solve_call(maps, ranks, lh, ll, xh, xl, fl, fr, op, panel, onext):
    any_spec = pl.BlockSpec(memory_space=pl.ANY)
    vmem = pl.BlockSpec(memory_space=pltpu.VMEM)
    dma = pltpu.SemaphoreType.DMA
    width = panel.shape[1]
    return pl.pallas_call(
        solve_kernel,
        out_shape=(
            jax.ShapeDtypeStruct(panel.shape, F32),
            jax.ShapeDtypeStruct(onext.shape, F32),
        ),
        in_specs=[pl.BlockSpec(memory_space=pltpu.SMEM)] * 2 + [any_spec] * 6 + [vmem] * 3,
        out_specs=(any_spec, any_spec),
        scratch_shapes=[
            pltpu.VMEM((N, N), BF16),
            pltpu.VMEM((N, N), BF16),
            pltpu.VMEM(fl.shape, BF16),
            pltpu.VMEM(op.shape, BF16),
            pltpu.VMEM(panel.shape, BF16),
            pltpu.VMEM(onext.shape, BF16),
            pltpu.VMEM((N, op.shape[1] + width), BF16),
            pltpu.VMEM((op.shape[1], N), BF16),
            pltpu.VMEM(panel.shape, F32),
            pltpu.VMEM(onext.shape, F32),
            dma((STEPS, 5)),
            dma(()),
            dma((STEPS + width // NB,)),
        ],
        compiler_params=pltpu.CompilerParams(vmem_limit_bytes=56 << 20),
        name="solve",
    )(maps, ranks, lh, ll, fl, op, panel, onext, xh, xl, fr)


def shards(fac_left, fac_right, block_rank, col_map, child_lead, orig_lead, orig_panel, orig_next):
    out_lead, lh, ll, xh, xl, flg, frg, opg = factor_call(
        child_lead[0], orig_lead[0], fac_left[0], fac_right[0], orig_panel[0]
    )
    upper, below = solve_call(col_map, block_rank, lh, ll, xh, xl, flg, frg, opg, orig_panel[0], orig_next[0])
    return (out_lead[None], upper[None], below[None])


def solution(mesh):
    placed = (
        P("leaf", None, "front"),
        P("leaf", None, "front"),
        P(),
        P(),
        P("leaf", "front", None),
        P("leaf", "front", None),
        P("leaf", None, "front"),
        P("leaf", None, "front"),
    )
    return jax.shard_map(
        shards,
        mesh=mesh,
        in_specs=placed,
        out_specs=(P("leaf", "front", None), P("leaf", None, "front"), P("leaf", None, "front")),
        check_vma=False,
    )
```
